32 devices in a mesh: pipe: 4 (over y, x), tensor: 8 (over z, core).
Axes of the slice: x: 2, y: 2, z: 4, core: 2. Of those that a mesh axis runs over, the one named last changes fastest.
Arguments:
- cotangent: bfloat16 [2, 128, 8192], P(None, 'tensor'), may hold values from -5 to 5
- inputs: bfloat16 [4, 2, 128, 8192], P('pipe', None, 'tensor'), may hold values from -24 to 24
- norm_gain: float32 [4, 8192], P('pipe'), may hold values from 0.1 to 1.9
- queries: bfloat16 [4, 2, 128, 4096], P('pipe', None, None, 'tensor'), may hold values from -4.6 to 4.6
- keys: bfloat16 [4, 2, 128, 4096], P('pipe', None, None, 'tensor'), may hold values from -4.6 to 4.6
- values: bfloat16 [4, 2, 128, 4096], P('pipe', None, None, 'tensor'), may hold values from -4 to 4
- qkv_weight: bfloat16 [4, 3, 8192, 4096], P('pipe', None, None, 'tensor'), may hold values from -0.0625 to 0.0625
- out_weight: bfloat16 [4, 4096, 8192], P('pipe', 'tensor'), may hold values from -0.09375 to 0.09375
- layout: int32 [2, 4, 4], replicated, may hold values from -1 to 3, as said below
Outputs:
- input_grads: bfloat16 [4, 2, 128, 8192], P('pipe', None, 'tensor')
The draws below stay inside these ranges and needn't reach their ends.
Inputs may be any that keep to these rules, and one draw needn't show every extreme that they name: `layout`: each entry is -1 (no block) or a key block not after its query block; the last entry of query block i is i and the one before it is i - 1 (or -1 for block 0); the first two entries are two blocks of the micro-batch that all later query blocks attend to.
All inputs are finite; a program needn't handle non-finite values.
Results may differ from the reference program's by a relative error of at most 0.02.
Values may be sent and summed in bfloat16 or wider, within the bound.
A program may use at most 128 MiB of HBM per device.

```python
import math
import jax
import jax.numpy as jnp
from jax import lax

D = 8192
HEADS = 32
HD = 128
SEQ = 128
MICRO = 2
BLOCK = 32
SECTIONS = 4
NB = 4
N_TENSOR = 8


def draw_queries(key, part):
    shape = (SECTIONS, MICRO, SEQ, HEADS * HD)
    base = jnp.clip(jax.random.normal(jax.random.fold_in(key, 1), shape, jnp.float32), -4.6, 4.6)
    return base.astype(jnp.bfloat16)


def draw_keys(key, part):
    shape = (SECTIONS, MICRO, SEQ, HEADS * HD)
    base = jnp.clip(jax.random.normal(jax.random.fold_in(key, 2), shape, jnp.float32), -4.6, 4.6)
    return base.astype(jnp.bfloat16)


def draw_inputs(key, part):
    shape = (SECTIONS, MICRO, SEQ, D)
    column_key, row_key, base_key = jax.random.split(key, 3)
    column_scale = jnp.exp(jax.random.uniform(column_key, (D,), jnp.float32, jnp.log(0.3), jnp.log(3.0)))
    row_scale = jnp.exp(jax.random.uniform(row_key, (SECTIONS, MICRO, SEQ, 1), jnp.float32, jnp.log(0.5), jnp.log(2.0)))
    base = jnp.clip(jax.random.normal(base_key, shape, jnp.float32), -4.0, 4.0)
    return (base * column_scale * row_scale).astype(jnp.bfloat16)


def draw_layout(key, part):
    first_key, second_key = jax.random.split(key)
    globals_one = jax.random.randint(first_key, (MICRO, 1), 0, NB)
    globals_two = jax.random.randint(second_key, (MICRO, 1), 0, NB)
    blocks = jnp.arange(NB, dtype=jnp.int32)[None, :]
    entry_one = jnp.where(globals_one <= blocks, globals_one, -1)
    entry_two = jnp.where(globals_two <= blocks, globals_two, -1)
    entry_prev = jnp.where(blocks >= 1, blocks - 1, -1)
    entry_self = jnp.broadcast_to(blocks, (MICRO, NB))
    return jnp.stack([entry_one, entry_two, jnp.broadcast_to(entry_prev, (MICRO, NB)), entry_self], -1).astype(jnp.int32)


def level_of(key, shape, cuts, low, high):
    def one(axis_at, shards_of):
        heights = jax.random.uniform(jax.random.fold_in(jax.random.fold_in(key, 6), axis_at), (shards_of,), jnp.float32, low / len(cuts), high / len(cuts))
        return jnp.repeat(jnp.exp(heights), shape[axis_at] // shards_of).reshape((-1,) + (1,) * (len(shape) - axis_at - 1))

    level = one(*cuts[0])
    for cut in cuts[1:]:
        level = level * one(*cut)
    return level


def noise(own_key, shape, width, most, cuts=(), kind=jnp.bfloat16):
    drawn = width * jax.random.normal(own_key, shape, jnp.float32)
    if cuts:
        drawn = drawn * level_of(own_key, shape, cuts, -0.22, 0.18)
    return jnp.clip(drawn, -most, most).astype(kind)


def setup_inputs(seed: int = 0) -> dict:
    arg_keys = jax.random.split(jax.random.key(seed), 10)
    cotangent = noise(arg_keys[0], (MICRO, SEQ, D), 1.0, 5.0, ((1, 8),))
    inputs = draw_inputs(jax.random.fold_in(arg_keys[9], 71), 0)
    norm_gain = jnp.clip(1.0 + 0.18 * jax.random.normal(arg_keys[2], (SECTIONS, D), jnp.float32), 0.1, 1.9)
    queries = draw_queries(jax.random.fold_in(arg_keys[9], 71), 0)
    keys = draw_keys(jax.random.fold_in(arg_keys[9], 71), 0)
    values = noise(arg_keys[5], (SECTIONS, MICRO, SEQ, HEADS * HD), 1.0, 4.0, ((0, 4), (3, 8)))
    qkv_weight = noise(arg_keys[6], (SECTIONS, 3, D, HEADS * HD), D ** -0.5, 0.0625, ((0, 4), (3, 8)))
    out_weight = noise(arg_keys[7], (SECTIONS, HEADS * HD, D), (HEADS * HD) ** -0.5, 0.09375, ((0, 4), (1, 8)))
    layout = draw_layout(jax.random.fold_in(arg_keys[9], 71), 0)
    return dict(cotangent=cotangent, inputs=inputs, norm_gain=norm_gain, queries=queries, keys=keys, values=values, qkv_weight=qkv_weight, out_weight=out_weight, layout=layout)


def block_mask(layout_rows):
    blocks = jnp.arange(NB, dtype=jnp.int32)
    listed = jnp.any(layout_rows[:, :, None] == blocks[None, None, :], axis=1)
    spread = jnp.broadcast_to(listed[:, None, :, None], (NB, BLOCK, NB, BLOCK)).reshape(SEQ, SEQ)
    places = jnp.arange(SEQ)
    return spread & (places[:, None] >= places[None, :])

def head_backward(query, key_rows, value_rows, out_grad, allowed):
    scale = 1.0 / math.sqrt(HD)
    scores = jnp.dot(query, key_rows.T, preferred_element_type=jnp.float32) * scale
    scores = jnp.where(allowed, scores, -1e+30)
    top = lax.optimization_barrier(jnp.max(scores, axis=1, keepdims=True))
    expo = jnp.exp(scores - top)
    probs = expo / lax.optimization_barrier(jnp.sum(expo, axis=1, keepdims=True))
    probs_half = probs.astype(jnp.bfloat16)
    attended = jnp.dot(probs_half, value_rows, preferred_element_type=jnp.float32)
    delta = lax.optimization_barrier(jnp.sum(out_grad.astype(jnp.float32) * attended, axis=1, keepdims=True))
    dprob = jnp.dot(out_grad, value_rows.T, preferred_element_type=jnp.float32)
    dscore = (probs * (dprob - delta)).astype(jnp.bfloat16)
    grad_query = (jnp.dot(dscore, key_rows, preferred_element_type=jnp.float32) * scale).astype(jnp.bfloat16)
    grad_key = (jnp.dot(dscore.T, query, preferred_element_type=jnp.float32) * scale).astype(jnp.bfloat16)
    grad_value = jnp.dot(probs_half.T, out_grad, preferred_element_type=jnp.float32).astype(jnp.bfloat16)
    return (grad_query, grad_key, grad_value)

def split_heads(array):
    return array.reshape(SEQ, HEADS, HD).transpose(1, 0, 2)

def join_heads(array):
    return array.transpose(1, 0, 2).reshape(SEQ, HEADS * HD)

def reference(cotangent, inputs, norm_gain, queries, keys, values, qkv_weight, out_weight, layout):
    groups = N_TENSOR
    columns = HEADS * HD // groups
    carried = [cotangent[micro] for micro in range(MICRO)]
    by_section = [None] * SECTIONS
    for section in range(SECTIONS - 1, -1, -1):
        produced = []
        for micro in range(MICRO):
            grad_rows = carried[micro]
            out_grad = jnp.dot(grad_rows, out_weight[section].T, preferred_element_type=jnp.float32).astype(jnp.bfloat16)
            allowed = block_mask(layout[micro])

            def per_head(items):
                return head_backward(items[0], items[1], items[2], items[3], allowed)
            grad_query, grad_key, grad_value = lax.map(per_head, (split_heads(queries[section, micro]), split_heads(keys[section, micro]), split_heads(values[section, micro]), split_heads(out_grad)))
            stacked = jnp.stack([join_heads(grad_query), join_heads(grad_key), join_heads(grad_value)], 0)
            weight = qkv_weight[section]

            def add_group(total, index):
                part = lax.dynamic_slice_in_dim(stacked, index * columns, columns, 2)
                weight_part = lax.dynamic_slice_in_dim(weight, index * columns, columns, 2)
                term = jnp.einsum('csn,cdn->sd', part.astype(jnp.float32), weight_part.astype(jnp.float32), precision=lax.Precision.HIGHEST)
                rounded = lax.optimization_barrier(term.astype(jnp.bfloat16))
                return (total + rounded.astype(jnp.float32), None)
            head_sum, _ = lax.scan(add_group, jnp.zeros((SEQ, D), jnp.float32), jnp.arange(groups, dtype=jnp.int32))
            x_rows = inputs[section, micro].astype(jnp.float32)
            factor = lax.rsqrt(lax.optimization_barrier(jnp.mean(x_rows * x_rows, axis=1, keepdims=True)) + 1e-05)
            normed = x_rows * factor
            scaled = head_sum * norm_gain[section][None, :]
            through = factor * (scaled - normed * lax.optimization_barrier(jnp.mean(scaled * normed, axis=1, keepdims=True)))
            produced.append((grad_rows.astype(jnp.float32) + through).astype(jnp.bfloat16))
        by_section[section] = jnp.stack(produced, 0)
        carried = produced
    return jnp.stack(by_section, 0)
```

```python
import functools
import math

import jax
import jax.numpy as jnp
from jax import lax
from jax.experimental import pallas as pl
from jax.experimental.pallas import tpu as pltpu
from jax.sharding import PartitionSpec as P

HD = 128
LANE = 128
MESH = pl.DeviceIdType.MESH
NT = (((1,), (1,)), ((), ()))
TN = (((0,), (0,)), ((), ()))
NN = (((1,), (0,)), ((), ()))


def mm(a, b, dims):
    return lax.dot_general(a, b, dims, preferred_element_type=jnp.float32)


def combos(dists):
    sets = [()]
    for d in dists:
        sets = sets + [s + (d,) for s in sets]
    return sets


def body(
    sizes,
    layout, cot, xs, gain, qs, ks, vs, wqkv_hbm, wout_hbm,
    out,
    wqkv, wout, xfull, full, part, sibs, zgot, gout, xst, xcol, rall, keep, ymat, acc,
    kacc, vacc, grads, probs_keep, att_keep, coef, dacc, dsend, coefin, coefown, ost, og,
    wout_sem, wqkv_sem, xh_s, xh_r, xa_s, xa_r, xs_s, xs_r, xc_s, xc_r, ra_s, ra_r,
    g_s, g_r, sg_s, sg_r, rb_s, rb_r, rz_s, rz_r, ci_s, ci_r, co_s, co_r, og_s, og_r,
):
    S, T, M, R, D, C, L, HV, KX = sizes
    Z = T // 2
    UR = L // HV
    NU = M * HV
    CK = T * LANE
    J = D // CK
    BR = UR // R
    XK = D // KX
    f32 = jnp.float32
    bf = jnp.bfloat16
    s = lax.axis_index("pipe")
    t = lax.axis_index("tensor")
    z = t // 2
    c = t % 2
    sib = z * 2 + (1 - c)
    scale = 1.0 / math.sqrt(HD)
    last = s == S - 1

    dists = []
    d = Z // 2
    while d >= 1:
        dists.append(d)
        d //= 2
    moves = []
    for i, d in enumerate(dists):
        moves.append((d, [(len(combos(dists[:i])) - 1 + n, s_) for n, s_ in enumerate(combos(dists[:i]))]))

    def flip(v, ds):
        for d in ds:
            v = v + d - 2 * d * ((v // d) % 2)
        return v

    def jcols(j):
        return pl.ds(pl.multiple_of(j * CK, CK), CK)

    def xcols(k):
        return pl.ds(pl.multiple_of(k * XK, XK), XK)

    def tile(j, o):
        return pl.ds(pl.multiple_of(j * CK + o * LANE, LANE), LANE)

    def remote(src, dst, ss, rs, device):
        return pltpu.make_async_remote_copy(
            src_ref=src, dst_ref=dst, send_sem=ss, recv_sem=rs,
            device_id=device, device_id_type=MESH,
        )

    def loop(n, fn):
        def step(i, carry):
            fn(i)
            return carry
        lax.fori_loop(0, n, step, 0)

    def other(dt):
        return lax.rem(t + dt, T)

    def source(dt):
        return lax.rem(t + (T - dt), T)

    def peer(dz):
        return lax.rem(z + dz, Z)

    def wout_copy(k):
        return pltpu.make_async_copy(wout_hbm.at[0, :, xcols(k)], wout.at[:, xcols(k)], wout_sem.at[k])

    def wqkv_copy(j):
        return pltpu.make_async_copy(
            wqkv_hbm.at[0, :, jcols(j), :], wqkv.at[:, jcols(j), :], wqkv_sem.at[j]
        )

    def xhop(m, section):
        return remote(xs.at[0, m], xfull.at[m, c, z], xh_s.at[m], xh_r.at[m], (section, t))

    def xmove(m, k, d, n, held):
        ref = xfull.at[m, c, flip(z, held), :, xcols(k)]
        return remote(ref, ref, xa_s.at[m, k, n], xa_r.at[m, k, n], (s, flip(z, (d,)) * 2 + c))

    def xmove_in(m, k, d, n, held):
        ref = xfull.at[m, c, flip(flip(z, (d,)), held), :, xcols(k)]
        return remote(ref, ref, xa_s.at[m, k, n], xa_r.at[m, k, n], (s, flip(z, (d,)) * 2 + c))

    def xsib(m, k):
        ref = xfull.at[m, c, :, :, xcols(k)]
        return remote(ref, ref, xs_s.at[m, k], xs_r.at[m, k], (s, sib))

    def xsib_in(m, k):
        ref = xfull.at[m, 1 - c, :, :, xcols(k)]
        return remote(ref, ref, xs_s.at[m, k], xs_r.at[m, k], (s, sib))

    def xc_out(m, dt):
        return remote(
            xst.at[other(dt), m], xcol.at[t, m], xc_s.at[m, dt - 1], xc_r.at[m, dt - 1], (s, other(dt))
        )

    def xc_in(m, dt):
        return remote(
            xst.at[other(dt), m], xcol.at[source(dt), m], xc_s.at[m, dt - 1], xc_r.at[m, dt - 1], (s, other(dt))
        )

    def ra_out(dt):
        return remote(rall.at[t], rall.at[t], ra_s.at[dt - 1], ra_r.at[dt - 1], (s, other(dt)))

    def ra_in(dt):
        o = source(dt)
        return remote(rall.at[o], rall.at[o], ra_s.at[dt - 1], ra_r.at[dt - 1], (s, other(dt)))

    def g_out(u, j, zz, section):
        return remote(
            gout.at[u, j], full.at[u, j, c, z], g_s.at[u, j, zz], g_r.at[u, j], (section, zz * 2 + c)
        )

    def g_in(u, j):
        ref = full.at[u, j, c]
        return remote(ref, ref, g_s.at[u, j, 0], g_r.at[u, j], (s, sib))

    def sg_out(u, j):
        ref = full.at[u, j, c]
        return remote(ref, ref, sg_s.at[u, j], sg_r.at[u, j], (s, sib))

    def sg_in(u, j):
        ref = full.at[u, j, 1 - c]
        return remote(ref, ref, sg_s.at[u, j], sg_r.at[u, j], (s, sib))

    def rb(u, j):
        return remote(part.at[u, j, 1 - c], sibs.at[u, j], rb_s.at[u, j], rb_r.at[u, j], (s, sib))

    def rz(u, j, dz):
        return remote(
            part.at[u, j, c, peer(dz)], zgot.at[u, j, dz - 1],
            rz_s.at[u, j, dz - 1], rz_r.at[u, j], (s, peer(dz) * 2 + c),
        )

    def rz_in(u, j):
        return remote(zgot.at[u, j], zgot.at[u, j], rz_s.at[u, j, 0], rz_r.at[u, j], (s, sib))

    def ci_out(u, o, section):
        return remote(dsend.at[u], coefin.at[u, t], ci_s.at[u, o], ci_r.at[u], (section, o))

    def ci_in(u):
        return remote(coefin.at[u], coefin.at[u], ci_s.at[u, 0], ci_r.at[u], (s, sib))

    def co_out(u, dt):
        return remote(dsend.at[u], coefown.at[u, dt - 1], co_s.at[u, dt - 1], co_r.at[u], (s, other(dt)))

    def co_in(u):
        return remote(coefown.at[u], coefown.at[u], co_s.at[u, 0], co_r.at[u], (s, sib))

    def og_out(u, i, dest):
        dt = lax.rem(dest + (T - t), T)
        return remote(ost.at[u, i], og.at[u // HV, dt - 1], og_s.at[u, i], og_r.at[u // HV], (s, dest))

    def og_in(m):
        return remote(og.at[m], og.at[m], og_s.at[0, 0], og_r.at[m], (s, sib))

    barrier = pltpu.get_barrier_semaphore()
    for dt in range(1, T):
        pl.semaphore_signal(barrier, inc=1, device_id=(s, other(dt)), device_id_type=MESH)

    @pl.when(s > 0)
    def _():
        for o in range(T):
            pl.semaphore_signal(barrier, inc=1, device_id=(s - 1, o), device_id_type=MESH)

    @pl.when(s < S - 1)
    def _():
        for o in range(T):
            pl.semaphore_signal(barrier, inc=1, device_id=(s + 1, o), device_id_type=MESH)

    loop(KX, lambda k: wout_copy(k).start())
    loop(J, lambda j: wqkv_copy(j).start())

    @pl.when(last)
    def _():
        for m in range(M):
            xfull[m, c, z] = cot[m]

    ends = jnp.where(s == 0, 1, 0) + jnp.where(s == S - 1, 1, 0)
    pl.semaphore_wait(barrier, T - 1 + T * (2 - ends))

    def move_start(m, i):
        d, pieces = moves[i]

        def one(k):
            if i > 0:
                before, arrived = moves[i - 1]
                for n, held in arrived:
                    xmove_in(m, k, before, n, held).wait_recv()
            for n, held in pieces:
                xmove(m, k, d, n, held).start()

        loop(KX, one)

    def move_end(m):
        before, arrived = moves[-1]

        def one(k):
            for n, held in arrived:
                xmove_in(m, k, before, n, held).wait_recv()
            xsib(m, k).start()

        loop(KX, one)

    def multiply(m):
        ymat[m] = jnp.zeros((L, C), f32)

        def one(k):
            @pl.when(m == 0)
            def _():
                wout_copy(k).wait()

            xsib_in(m, k).wait_recv()
            rows = jnp.concatenate([xfull[m, o % 2, o // 2, :, xcols(k)] for o in range(T)], axis=0)
            ymat[m] += mm(rows, wout[:, xcols(k)], NT)

        loop(KX, one)

    @pl.when(last)
    def _():
        move_start(0, 0)

    @pl.when(s > 0)
    def _():
        for m in range(M):
            xhop(m, s - 1).start()

    for m in range(M):
        def square(k, carry):
            x = xs[0, m, :, xcols(k)].astype(f32)
            return carry + jnp.sum(x * x, axis=1, keepdims=True)

        squares = lax.fori_loop(0, KX, square, jnp.zeros((R, 1), f32))
        rall[t, m] = jnp.broadcast_to(lax.rsqrt(squares / D + 1e-05), (R, LANE))

        def stage(j):
            for o in range(T):
                xst[o, m, j] = xs[0, m, :, tile(j, o)]

        loop(J, stage)
    xcol[t] = xst[t]

    def send_cols(m):
        for dt in range(1, T):
            xc_out(m, dt).start()

    @pl.when(last)
    def _():
        for i in range(1, len(moves)):
            move_start(0, i)
        move_end(0)

    for dt in range(1, T):
        ra_out(dt).start()
    for m in range(M):
        send_cols(m)

    @pl.when(last)
    def _():
        multiply(0)
        for m in range(1, M):
            move_start(m, 0)

    @pl.when(s < S - 1)
    def _():
        for m in range(M):
            xhop(m, s).wait_recv()
            for i in range(len(moves)):
                move_start(m, i)
        for m in range(M):
            move_end(m)
            multiply(m)

    for dt in range(1, T):
        ra_in(dt).wait_recv()
        for m in range(M):
            xc_in(m, dt).wait_recv()

    def rows_of(u):
        return (HV - 1 - u % HV)

    def column(tile8):
        return jnp.transpose(jnp.broadcast_to(tile8[0:1], (LANE, LANE)))[:UR]

    def lanes(col):
        wide = jnp.broadcast_to(col, (UR, LANE))
        if UR < LANE:
            wide = jnp.concatenate([wide, jnp.zeros((LANE - UR, LANE), f32)], axis=0)
        return jnp.transpose(wide)[0:8]

    def xtile(u, j):
        src = rows_of(u) * BR
        return xcol[pl.ds(src, BR), u // HV, j].reshape(UR, LANE).astype(f32)

    def factors(u):
        src = rows_of(u) * BR
        return rall[pl.ds(src, BR), u // HV].reshape(UR, LANE)

    def give(u):
        co_in(u).wait_recv()
        total = dsend[u]
        for dt in range(1, T):
            total = total + coefown[u, dt - 1]
        cc = column(total)
        m = u // HV

        def one(j):
            value = (keep[u, j] - cc * xtile(u, j)).astype(bf)
            for i in range(BR):
                ost[u, i, j] = value[i * R : (i + 1) * R]

        loop(J, one)
        for i in range(BR):
            dest = rows_of(u) * BR + i

            @pl.when(dest != t)
            def _():
                og_out(u, i, dest).start()

            @pl.when(dest == t)
            def _():
                def own(j):
                    out[m, :, tile(j, t)] = ost[u, i, j]

                loop(J, own)

    def unit(u):
        m = u // HV
        half = rows_of(u)
        r0 = pl.multiple_of(half * UR, UR)
        rows = pl.ds(r0, UR)

        @pl.when(last & (u % HV == 0) & (m > 0))
        def _():
            move_end(m)
            multiply(m)

        nb = layout.shape[1]
        bl = L // nb
        kb = lax.broadcasted_iota(jnp.int32, (bl, L), 1) // bl
        strips = []
        for b in range(nb // HV):
            at = half * (nb // HV) + b
            strip = kb == layout[m, at, 0]
            for e in range(1, layout.shape[2]):
                strip = strip | (kb == layout[m, at, e])
            strips.append(jnp.where(strip, 1.0, 0.0))
        listed = jnp.concatenate(strips, axis=0)
        row = lax.broadcasted_iota(jnp.int32, (UR, L), 0) + r0
        col = lax.broadcasted_iota(jnp.int32, (UR, L), 1)
        allowed = (listed > 0.5) & (col <= row)
        for h in range(C // HD):
            hc = slice(h * HD, (h + 1) * HD)
            scores = jnp.where(allowed, mm(qs[m, rows, hc], ks[m, :, hc], NT) * scale, -1e30)
            expo = jnp.exp(scores - jnp.max(scores, axis=1, keepdims=True))
            probs = expo / jnp.sum(expo, axis=1, keepdims=True)
            probs_keep[h] = probs
            att_keep[:, hc] = mm(probs.astype(bf), vs[m, :, hc], NN)

        acc[...] = jnp.zeros_like(acc)
        coef[...] = jnp.full((UR, LANE), -1.0, f32)

        @pl.when(s < S - 1)
        def _():
            def gather(i):
                @pl.when(i < J)
                def _():
                    g_in(u, i).wait_recv()
                    sg_out(u, i).start()

                @pl.when(i > 0)
                def _():
                    j = i - 1
                    sg_in(u, j).wait_recv()
                    wide = jnp.concatenate([full[u, j, o % 2, o // 2] for o in range(T)], axis=1)
                    acc[...] += mm(wide, wout[:, jcols(j)], NT)

            loop(J + 1, gather)
            ci_in(u).wait_recv()
            total = coefin[u, 0]
            for o in range(1, T):
                total = total + coefin[u, o]
            coef[...] = column(total)

        first = u % HV == 0
        for h in range(C // HD):
            hc = slice(h * HD, (h + 1) * HD)
            query = qs[m, rows, hc]
            key = ks[m, :, hc]
            value = vs[m, :, hc]
            go = (acc[:, hc] - coef[...] * ymat[m, rows, hc]).astype(bf)
            probs = probs_keep[h]
            delta = jnp.sum(att_keep[:, hc] * go.astype(f32), axis=1, keepdims=True)
            dprob = mm(go, value, NT)
            dscore = (probs * (dprob - delta)).astype(bf)
            grads[0, :, hc] = (mm(dscore, key, NN) * scale).astype(bf)
            gk = mm(dscore, query, TN)
            gv = mm(probs.astype(bf), go, TN)
            if HV > 1:
                kacc[:, hc] = jnp.where(first, 0.0, kacc[:, hc]) + gk
                vacc[:, hc] = jnp.where(first, 0.0, vacc[:, hc]) + gv
                grads[1, :, hc] = (kacc[rows, hc] * scale).astype(bf)
                grads[2, :, hc] = vacc[rows, hc].astype(bf)
            else:
                grads[1, :, hc] = (gk * scale).astype(bf)
                grads[2, :, hc] = gv.astype(bf)

        dacc[...] = jnp.zeros_like(dacc)

        def produce(j):
            @pl.when(u == 0)
            def _():
                wqkv_copy(j).wait()

            cols = jcols(j)
            value = mm(grads[0], wqkv[0, cols, :], NT)
            value = value + mm(grads[1], wqkv[1, cols, :], NT)
            value = value + mm(grads[2], wqkv[2, cols, :], NT)
            value = value.astype(bf)
            for o in range(T):
                part[u, j, o % 2, o // 2] = value[:, o * LANE : (o + 1) * LANE]
            rb(u, j).start()

        def pair(j):
            rb(u, j).wait_recv()
            part[u, j, c] = (part[u, j, c].astype(f32) + sibs[u, j].astype(f32)).astype(bf)
            for dz in range(1, Z):
                rz(u, j, dz).start()

        def finish(j):
            rz_in(u, j).wait_recv()
            total = part[u, j, c, z].astype(f32)
            for dz in range(1, Z):
                total = total + zgot[u, j, dz - 1].astype(f32)
            at = tile(j, t)
            scaled = total * gain[:, at]
            above = jnp.concatenate(
                [xfull[m, i % 2, half * (BR // 2) + i // 2, :, at] for i in range(BR)], axis=0
            ).astype(f32)
            came = jnp.where(last, 0.0, full[u, j, c, z].astype(f32))
            value = came - coef[...] * above + factors(u) * scaled
            keep[u, j] = value

            @pl.when(s > 0)
            def _():
                gout[u, j] = value.astype(bf)
                for zz in range(Z):
                    g_out(u, j, zz, s - 1).start()

            dacc[...] += scaled * xtile(u, j)

        P1, P2 = 2, 5

        def step(i):
            @pl.when(i < J)
            def _():
                produce(i)

            @pl.when((i >= P1) & (i < J + P1))
            def _():
                pair(i - P1)

            @pl.when(i >= P2)
            def _():
                finish(i - P2)

        loop(J + P2, step)

        rr = factors(u)
        dsend[u] = lanes(jnp.sum(dacc[...], axis=1, keepdims=True) * rr * rr * (1.0 / D))

        @pl.when(s > 0)
        def _():
            for o in range(T):
                ci_out(u, o, s - 1).start()

        for dt in range(1, T):
            co_out(u, dt).start()

        @pl.when(last & (u % HV == 0) & (m + 1 < M))
        def _():
            for i in range(1, len(moves)):
                move_start(m + 1, i)

        @pl.when(u > 0)
        def _():
            give(u - 1)

    loop(NU, unit)
    give(NU - 1)

    for m in range(M):
        og_in(m).wait_recv()
        for dt in range(1, T):
            def place(j):
                out[m, :, tile(j, source(dt))] = og[m, dt - 1, j]

            loop(J, place)

    @pl.when(s > 0)
    def _():
        for m in range(M):
            xhop(m, s - 1).wait_send()

    for dt in range(1, T):
        ra_out(dt).wait_send()

    def drain_m(m):
        def drain_k(k):
            for d, pieces in moves:
                for n, held in pieces:
                    xmove(m, k, d, n, held).wait_send()
            xsib(m, k).wait_send()

        loop(KX, drain_k)
        for dt in range(1, T):
            xc_out(m, dt).wait_send()

    loop(M, drain_m)

    def drain_u(u):
        def drain_j(j):
            rb(u, j).wait_send()
            for dz in range(1, Z):
                rz(u, j, dz).wait_send()

            @pl.when(s < S - 1)
            def _():
                sg_out(u, j).wait_send()

            @pl.when(s > 0)
            def _():
                for zz in range(Z):
                    g_out(u, j, zz, s - 1).wait_send()

        loop(J, drain_j)

        @pl.when(s > 0)
        def _():
            for o in range(T):
                ci_out(u, o, s - 1).wait_send()

        for dt in range(1, T):
            co_out(u, dt).wait_send()
        for i in range(BR):
            dest = rows_of(u) * BR + i

            @pl.when(dest != t)
            def _():
                og_out(u, i, dest).wait_send()

    loop(NU, drain_u)


def solution(mesh):
    S = mesh.shape["pipe"]
    T = mesh.shape["tensor"]

    def shards(cotangent, inputs, norm_gain, queries, keys, values, qkv_weight, out_weight, layout):
        M, R, D = cotangent.shape
        C = queries.shape[3]
        L = queries.shape[2]
        Z = T // 2
        HV = 2
        KX = 4
        UR = L // HV
        NU = M * HV
        J = D // (T * LANE)
        BR = UR // R
        sizes = (S, T, M, R, D, C, L, HV, KX)
        vmem = pl.BlockSpec(memory_space=pltpu.VMEM)
        hbm = pl.BlockSpec(memory_space=pl.ANY)
        bf = jnp.bfloat16
        f32 = jnp.float32
        dma = pltpu.SemaphoreType.DMA
        V = pltpu.VMEM
        result = pl.pallas_call(
            functools.partial(body, sizes),
            out_shape=jax.ShapeDtypeStruct((M, R, D), bf),
            in_specs=[pl.BlockSpec(memory_space=pltpu.SMEM)] + [vmem] * 6 + [hbm] * 2,
            out_specs=vmem,
            scratch_shapes=[
                V((3, D, C), bf),
                V((C, D), bf),
                V((M, 2, Z, R, D), bf),
                V((NU, J, 2, Z, UR, LANE), bf),
                V((NU, J, 2, Z, UR, LANE), bf),
                V((NU, J, Z, UR, LANE), bf),
                V((NU, J, Z - 1, UR, LANE), bf),
                V((NU, J, UR, LANE), bf),
                V((T, M, J, R, LANE), bf),
                V((T, M, J, R, LANE), bf),
                V((T, M, R, LANE), f32),
                V((NU, J, UR, LANE), f32),
                V((M, L, C), f32),
                V((UR, C), f32),
                V((L, C), f32),
                V((L, C), f32),
                V((3, UR, C), bf),
                V((C // HD, UR, L), f32),
                V((UR, C), f32),
                V((UR, LANE), f32),
                V((UR, LANE), f32),
                V((NU, 8, LANE), f32),
                V((NU, T, 8, LANE), f32),
                V((NU, T - 1, 8, LANE), f32),
                V((NU, BR, J, R, LANE), bf),
                V((M, T - 1, J, R, LANE), bf),
                dma((KX,)),
                dma((J,)),
                dma((M,)),
                dma((M,)),
                dma((M, KX, Z - 1)),
                dma((M, KX, Z - 1)),
                dma((M, KX)),
                dma((M, KX)),
                dma((M, T - 1)),
                dma((M, T - 1)),
                dma((T - 1,)),
                dma((T - 1,)),
                dma((NU, J, Z)),
                dma((NU, J)),
                dma((NU, J)),
                dma((NU, J)),
                dma((NU, J)),
                dma((NU, J)),
                dma((NU, J, Z - 1)),
                dma((NU, J)),
                dma((NU, T)),
                dma((NU,)),
                dma((NU, T - 1)),
                dma((NU,)),
                dma((NU, BR)),
                dma((M,)),
            ],
            compiler_params=pltpu.CompilerParams(
                collective_id=0, has_side_effects=True, vmem_limit_bytes=62 * 1024 * 1024
            ),
        )(
            layout, cotangent, inputs, norm_gain, queries[0], keys[0], values[0],
            qkv_weight, out_weight,
        )
        return result[None]

    in_specs = (
        P(None, "tensor", None),
        P("pipe", None, "tensor", None),
        P("pipe", None),
        P("pipe", None, None, "tensor"),
        P("pipe", None, None, "tensor"),
        P("pipe", None, None, "tensor"),
        P("pipe", None, None, "tensor"),
        P("pipe", "tensor", None),
        P(),
    )
    out_specs = P("pipe", None, "tensor", None)
    return jax.shard_map(shards, mesh=mesh, in_specs=in_specs, out_specs=out_specs, check_vma=False)
```

```python
import functools
import math

import jax
import jax.numpy as jnp
from jax import lax
from jax.experimental import pallas as pl
from jax.experimental.pallas import tpu as pltpu
from jax.sharding import PartitionSpec as P

HD = 128
LANE = 128
MESH = pl.DeviceIdType.MESH
NT = (((1,), (1,)), ((), ()))
TN = (((0,), (0,)), ((), ()))
NN = (((1,), (0,)), ((), ()))


def mm(a, b, dims):
    return lax.dot_general(a, b, dims, preferred_element_type=jnp.float32)


def combos(dists):
    sets = [()]
    for d in dists:
        sets = sets + [s + (d,) for s in sets]
    return sets


def body(
    sizes,
    layout, cot, xs, gain, qs, ks, vs, wqkv_hbm, wout_hbm,
    out,
    wqkv, wout, xfull, full, part, sibs, zgot, gout, keep, ymat, acc,
    grads, probs_keep, att_keep, coef, factor, dacc, dsend, coefin,
    wout_sem, wqkv_sem, ln_s, xh_s, xh_r, xa_s, xa_r, xs_s, xs_r,
    hop_s, hop_r, g_s, g_r, sg_s, sg_r, rb_s, rb_r, rz_s, rz_r, ci_s, ci_r,
):
    S, T, M, R, D, C, L, J, KX, KA, DIRECT, SKEW = sizes
    Z = T // 2
    CK = D // J
    XK = D // KX
    f32 = jnp.float32
    bf = jnp.bfloat16
    s = lax.axis_index("pipe")
    t = lax.axis_index("tensor")
    z = t // 2
    c = t % 2
    sib = z * 2 + (1 - c)
    scale = 1.0 / math.sqrt(HD)
    last = s == S - 1

    dists = []
    d = Z // 2
    while d >= 1:
        dists.append(d)
        d //= 2
    moves = []
    for i, d in enumerate(dists):
        held = combos(dists[:i])
        moves.append((d, [(len(held) - 1 + n, h) for n, h in enumerate(held)]))
    halves = []
    count = 0
    up = dists[::-1]
    for i, d in enumerate(up):
        held = combos(up[i + 1 :])
        halves.append((d, [(count + n, h) for n, h in enumerate(held)]))
        count += len(held)
    spans = [(n, (d,) + held) for d, pieces in moves for n, held in pieces]
    if DIRECT:
        gmoves = [[(n, ds, ()) for n, ds in spans]]
    else:
        gmoves = [[(n, (d,), held) for n, held in pieces] for d, pieces in moves]

    def flip(v, ds):
        for d in ds:
            v = v + d - 2 * d * ((v // d) % 2)
        return v

    def jcols(j):
        return pl.ds(pl.multiple_of(j * CK, CK), CK)

    def xcols(k):
        return pl.ds(pl.multiple_of(k * XK, XK), XK)

    def remote(src, dst, ss, rs, device):
        return pltpu.make_async_remote_copy(
            src_ref=src, dst_ref=dst, send_sem=ss, recv_sem=rs,
            device_id=device, device_id_type=MESH,
        )

    def loop(n, fn):
        def step(i, carry):
            fn(i)
            return carry
        lax.fori_loop(0, n, step, 0)

    def wout_copy(k):
        return pltpu.make_async_copy(wout_hbm.at[0, :, xcols(k)], wout.at[:, xcols(k)], wout_sem.at[k])

    def wqkv_copy(j):
        return pltpu.make_async_copy(
            wqkv_hbm.at[0, :, jcols(j), :], wqkv.at[:, jcols(j), :], wqkv_sem.at[j]
        )

    def xhop(m, section):
        return remote(xs.at[0, m], xfull.at[m, c, z], xh_s.at[m], xh_r.at[m], (section, t))

    def xmove(m, k, d, n, held):
        ref = xfull.at[m, c, flip(z, held), :, xcols(k)]
        return remote(ref, ref, xa_s.at[m, k, n], xa_r.at[m, k, n], (s, flip(z, (d,)) * 2 + c))

    def xmove_in(m, k, d, n, held):
        ref = xfull.at[m, c, flip(flip(z, (d,)), held), :, xcols(k)]
        return remote(ref, ref, xa_s.at[m, k, n], xa_r.at[m, k, n], (s, flip(z, (d,)) * 2 + c))

    def lend(m, k, n, ds):
        return remote(
            cot.at[m, :, xcols(k)], xfull.at[m, c, z, :, xcols(k)],
            ln_s.at[m, k, n], xa_r.at[m, k, n], (S - 1, flip(z, ds) * 2 + c),
        )

    def lent(m, k):
        return last & ((m > 0) | (k >= KA))

    def lends(m, k):
        if m > 0:
            return S - 3
        return S - 2 - k % 2

    def xsib(m, k):
        ref = xfull.at[m, c, :, :, xcols(k)]
        return remote(ref, ref, xs_s.at[m, k], xs_r.at[m, k], (s, sib))

    def xsib_in(m, k):
        ref = xfull.at[m, 1 - c, :, :, xcols(k)]
        return remote(ref, ref, xs_s.at[m, k], xs_r.at[m, k], (s, sib))

    def hop(u, j, section):
        return remote(
            gout.at[u, j], full.at[u, j, c, z], hop_s.at[u, j], hop_r.at[u, j], (section, t)
        )

    def gmove(u, j, n, ds, held):
        ref = full.at[u, j, c, flip(z, held)]
        return remote(ref, ref, g_s.at[u, j, n], g_r.at[u, j, n], (s, flip(z, ds) * 2 + c))

    def gmove_in(u, j, n, ds, held):
        ref = full.at[u, j, c, flip(flip(z, ds), held)]
        return remote(ref, ref, g_s.at[u, j, n], g_r.at[u, j, n], (s, flip(z, ds) * 2 + c))

    def sg_out(u, j):
        ref = full.at[u, j, c]
        return remote(ref, ref, sg_s.at[u, j], sg_r.at[u, j], (s, sib))

    def sg_in(u, j):
        ref = full.at[u, j, 1 - c]
        return remote(ref, ref, sg_s.at[u, j], sg_r.at[u, j], (s, sib))

    def rb(u, j):
        return remote(part.at[u, j, 1 - c], sibs.at[u, j], rb_s.at[u, j], rb_r.at[u, j], (s, sib))

    def rz(u, j, d, n, held):
        q = flip(z, (d,))
        return remote(
            part.at[u, j, c, flip(q, held)], zgot.at[u, j, n],
            rz_s.at[u, j, n], rz_r.at[u, j, n], (s, q * 2 + c),
        )

    def ci_out(u, o, section):
        return remote(dsend.at[u], coefin.at[u, t], ci_s.at[u, o], ci_r.at[u], (section, o))

    def ci_in(u):
        return remote(coefin.at[u], coefin.at[u], ci_s.at[u, 0], ci_r.at[u], (s, sib))

    barrier = pltpu.get_barrier_semaphore()
    for dt in range(1, T):
        pl.semaphore_signal(barrier, inc=1, device_id=(s, lax.rem(t + dt, T)), device_id_type=MESH)

    @pl.when(s > 0)
    def _():
        for o in range(T):
            pl.semaphore_signal(barrier, inc=1, device_id=(s - 1, o), device_id_type=MESH)

    @pl.when(s < S - 1)
    def _():
        for o in range(T):
            pl.semaphore_signal(barrier, inc=1, device_id=(s + 1, o), device_id_type=MESH)

    @pl.when(last)
    def _():
        for o in range(T):
            pl.semaphore_signal(barrier, inc=1, device_id=(S - 3, o), device_id_type=MESH)

    loop(KX, lambda k: wout_copy(k).start())
    loop(J, lambda j: wqkv_copy(j).start())

    @pl.when(last)
    def _():
        for m in range(M):
            xfull[m, c, z] = cot[m]

    ends = jnp.where(s == 0, 1, 0) + jnp.where(s == S - 1, 1, 0)
    pl.semaphore_wait(barrier, T - 1 + T * (2 - ends) + jnp.where(s == S - 3, T, 0))

    def move_start(m, i):
        d, pieces = moves[i]

        def one(k):
            @pl.when(~lent(m, k))
            def _():
                if i > 0:
                    before, arrived = moves[i - 1]
                    for n, held in arrived:
                        xmove_in(m, k, before, n, held).wait_recv()
                for n, held in pieces:
                    xmove(m, k, d, n, held).start()

        loop(KX, one)

    def move_end(m):
        before, arrived = moves[-1]

        def one(k):
            for n, held in arrived:
                xmove_in(m, k, before, n, held).wait_recv()

            @pl.when(lent(m, k))
            def _():
                for d, pieces in moves[:-1]:
                    for n, held in pieces:
                        xmove_in(m, k, d, n, held).wait_recv()

            xsib(m, k).start()

        loop(KX, one)

    def multiply(m):
        ymat[m] = jnp.zeros((L, C), f32)

        def one(k):
            @pl.when(m == 0)
            def _():
                wout_copy(k).wait()

            xsib_in(m, k).wait_recv()
            rows = jnp.concatenate([xfull[m, o % 2, o // 2, :, xcols(k)] for o in range(T)], axis=0)
            ymat[m] += mm(rows, wout[:, xcols(k)], NT)

        loop(KX, one)

    def lending(fn):
        for m in range(M):
            for k in range(KX):
                if m > 0 or k >= KA:
                    @pl.when(s == lends(m, k))
                    def _():
                        for n, ds in spans:
                            fn(m, k, n, ds)

    @pl.when(last)
    def _():
        move_start(0, 0)

    lending(lambda m, k, n, ds: lend(m, k, n, ds).start())

    @pl.when(s > 0)
    def _():
        for m in range(M):
            xhop(m, s - 1).start()

    for m in range(M):
        def square(k, carry):
            x = xs[0, m, :, xcols(k)].astype(f32)
            return carry + jnp.sum(x * x, axis=1, keepdims=True)

        squares = lax.fori_loop(0, KX, square, jnp.zeros((R, 1), f32))
        factor[m] = jnp.broadcast_to(lax.rsqrt(squares / D + 1e-05), (R, LANE))

    @pl.when(last)
    def _():
        for i in range(1, len(moves)):
            move_start(0, i)
        move_end(0)
        multiply(0)

    @pl.when(s < S - 1)
    def _():
        for m in range(M):
            xhop(m, s).wait_recv()
            move_start(m, 0)
        for i in range(1, len(moves)):
            for m in range(M):
                move_start(m, i)
        move_end(0)
        multiply(0)

    @pl.when(s < S - 2)
    def _():
        for m in range(1, M):
            move_end(m)
            multiply(m)

    def prepare(u):
        nb = layout.shape[1]
        bl = L // nb
        kb = lax.broadcasted_iota(jnp.int32, (bl, L), 1) // bl
        strips = []
        for b in range(nb):
            strip = kb == layout[u, b, 0]
            for e in range(1, layout.shape[2]):
                strip = strip | (kb == layout[u, b, e])
            strips.append(jnp.where(strip, 1.0, 0.0))
        listed = jnp.concatenate(strips, axis=0)
        row = lax.broadcasted_iota(jnp.int32, (L, L), 0)
        col = lax.broadcasted_iota(jnp.int32, (L, L), 1)
        allowed = (listed > 0.5) & (col <= row)
        for h in range(C // HD):
            hc = slice(h * HD, (h + 1) * HD)
            scores = jnp.where(allowed, mm(qs[u, :, hc], ks[u, :, hc], NT) * scale, -1e30)
            expo = jnp.exp(scores - jnp.max(scores, axis=1, keepdims=True))
            probs = expo / jnp.sum(expo, axis=1, keepdims=True)
            probs_keep[u % 2, h] = probs
            att_keep[u % 2, :, hc] = mm(probs.astype(bf), vs[u, :, hc], NN)

    def attend(u):
        @pl.when(last)
        def _():
            coef[...] = jnp.full((L, LANE), -1.0, f32)

        @pl.when(s < S - 1)
        def _():
            ci_in(u).wait_recv()
            coef[...] = jnp.concatenate([coefin[u, o] for o in range(T)], axis=0)

        for h in range(C // HD):
            hc = slice(h * HD, (h + 1) * HD)
            query = qs[u, :, hc]
            key = ks[u, :, hc]
            value = vs[u, :, hc]
            go = (acc[:, hc] - coef[...] * ymat[u, :, hc]).astype(bf)
            probs = probs_keep[u % 2, h]
            delta = jnp.sum(att_keep[u % 2, :, hc] * go.astype(f32), axis=1, keepdims=True)
            dprob = mm(go, value, NT)
            dscore = (probs * (dprob - delta)).astype(bf)
            grads[0, :, hc] = (mm(dscore, key, NN) * scale).astype(bf)
            grads[1, :, hc] = (mm(dscore, query, TN) * scale).astype(bf)
            grads[2, :, hc] = mm(probs.astype(bf), go, TN).astype(bf)
        dacc[...] = jnp.zeros_like(dacc)

    def produce(u, j):
        @pl.when(u == 0)
        def _():
            wqkv_copy(j).wait()

        cols = jcols(j)
        value = mm(grads[0], wqkv[0, cols, :], NT)
        value = value + mm(grads[1], wqkv[1, cols, :], NT)
        value = value + mm(grads[2], wqkv[2, cols, :], NT)
        value = value.astype(bf)
        for o in range(T):
            part[u, j, o % 2, o // 2] = value[o * R : (o + 1) * R]
        rb(u, j).start()

    def combine(u, j, i):
        if i == 0:
            rb(u, j).wait_recv()
            part[u, j, c] = (part[u, j, c].astype(f32) + sibs[u, j].astype(f32)).astype(bf)
        else:
            before, arrived = halves[i - 1]
            for n, held in arrived:
                rz(u, j, before, n, held).wait_recv()
            for n, held in arrived:
                if held:
                    at = flip(z, held)
                    total = part[u, j, c, at].astype(f32) + zgot[u, j, n].astype(f32)
                    part[u, j, c, at] = total.astype(bf)
        d, pieces = halves[i]
        for n, held in pieces:
            rz(u, j, d, n, held).start()

    def finish(u, j):
        before, arrived = halves[-1]
        for n, held in arrived:
            rz(u, j, before, n, held).wait_recv()
        cols = jcols(j)
        total = part[u, j, c, z].astype(f32)
        for d, pieces in halves:
            total = total + zgot[u, j, pieces[0][0]].astype(f32)
        scaled = total * gain[:, cols]
        mine = coef[pl.ds(pl.multiple_of(t * R, R), R), :][:, 0:1]
        above = xfull[u, c, z, :, cols].astype(f32)
        came = jnp.where(last, 0.0, full[u, j, c, z].astype(f32))
        value = came - mine * above + factor[u][:, 0:1] * scaled
        keep[u, :, cols] = value

        @pl.when(s > 0)
        def _():
            gout[u, j] = value.astype(bf)
            hop(u, j, s - 1).start()

        product = scaled * xs[0, u, :, cols].astype(f32)
        sums = product[:, 0:LANE]
        for i in range(1, CK // LANE):
            sums = sums + product[:, i * LANE : (i + 1) * LANE]
        dacc[...] += sums

    def settle(u):
        r = factor[u]
        dots = jnp.sum(dacc[...], axis=1, keepdims=True)
        dsend[u] = r * r * dots * (1.0 / D)

        @pl.when(s > 0)
        def _():
            for o in range(T):
                ci_out(u, o, s - 1).start()

    def give(u):
        cc = dsend[u][:, 0:1]

        def one(j):
            cols = jcols(j)
            out[u, :, cols] = (keep[u, :, cols] - cc * xs[0, u, :, cols].astype(f32)).astype(bf)

        loop(J, one)

    def spread(u, j, i):
        if i == 0:
            hop(u, j, s).wait_recv()
        else:
            for move in gmoves[i - 1]:
                gmove_in(u, j, *move).wait_recv()
        if i < len(gmoves):
            for move in gmoves[i]:
                gmove(u, j, *move).start()
        else:
            sg_out(u, j).start()

    def project(u, j):
        sg_in(u, j).wait_recv()
        rows = jnp.concatenate([full[u, j, o % 2, o // 2] for o in range(T)], axis=0)
        acc[...] += mm(rows, wout[:, jcols(j)], NT)

    P1, PD, Q0, QD = SKEW
    PE = P1 + PD * len(halves)
    QE = Q0 + QD * (len(gmoves) + 1)

    def merged(n):
        u = n - 1
        mine = u >= 0
        more = u + 1 < M

        @pl.when((s >= S - 2) & (u > 0))
        def _():
            multiply(u)

        @pl.when(mine)
        def _():
            attend(u)

        acc[...] = jnp.zeros_like(acc)

        def step(i):
            def on(skew):
                return (i >= skew) & (i < J + skew)

            @pl.when(mine)
            def _():
                @pl.when(i < J)
                def _():
                    produce(u, i)

                for k in range(len(halves)):
                    @pl.when(on(P1 + PD * k))
                    def _():
                        combine(u, i - (P1 + PD * k), k)

                @pl.when(on(PE))
                def _():
                    finish(u, i - PE)

                @pl.when(i == J + PE - 1)
                def _():
                    settle(u)
                    give(u)

            @pl.when(more & (i == jnp.where(mine, J, 0)))
            def _():
                prepare(u + 1)

            @pl.when(more & (s < S - 1))
            def _():
                for k in range(len(gmoves) + 1):
                    @pl.when(on(Q0 + QD * k))
                    def _():
                        spread(u + 1, i - (Q0 + QD * k), k)

                @pl.when(on(QE))
                def _():
                    project(u + 1, i - QE)

        loop(J + max(QE, PE), step)

        @pl.when((s >= S - 2) & mine & more)
        def _():
            move_end(u + 1)

    loop(M + 1, merged)

    lending(lambda m, k, n, ds: lend(m, k, n, ds).wait_send())

    @pl.when(s > 0)
    def _():
        for m in range(M):
            xhop(m, s - 1).wait_send()

    def drain(m):
        def drain_k(k):
            @pl.when(~lent(m, k))
            def _():
                for d, pieces in moves:
                    for n, held in pieces:
                        xmove(m, k, d, n, held).wait_send()

            xsib(m, k).wait_send()

        loop(KX, drain_k)

        def drain_j(j):
            rb(m, j).wait_send()
            for d, pieces in halves:
                for n, held in pieces:
                    rz(m, j, d, n, held).wait_send()

            @pl.when(s < S - 1)
            def _():
                for moved in gmoves:
                    for move in moved:
                        gmove(m, j, *move).wait_send()
                sg_out(m, j).wait_send()

            @pl.when(s > 0)
            def _():
                hop(m, j, s - 1).wait_send()

        loop(J, drain_j)

        @pl.when(s > 0)
        def _():
            for o in range(T):
                ci_out(m, o, s - 1).wait_send()

    loop(M, drain)


def solution(mesh):
    S = mesh.shape["pipe"]
    T = mesh.shape["tensor"]

    def shards(cotangent, inputs, norm_gain, queries, keys, values, qkv_weight, out_weight, layout):
        M, R, D = cotangent.shape
        C = queries.shape[3]
        L = queries.shape[2]
        Z = T // 2
        J = 8
        KX = 4
        KA = 2
        DIRECT = False
        SKEW = (2, 2, 12, 2)
        CK = D // J
        sizes = (S, T, M, R, D, C, L, J, KX, KA, DIRECT, SKEW)
        vmem = pl.BlockSpec(memory_space=pltpu.VMEM)
        hbm = pl.BlockSpec(memory_space=pl.ANY)
        bf = jnp.bfloat16
        f32 = jnp.float32
        dma = pltpu.SemaphoreType.DMA
        V = pltpu.VMEM
        result = pl.pallas_call(
            functools.partial(body, sizes),
            out_shape=jax.ShapeDtypeStruct((M, R, D), bf),
            in_specs=[pl.BlockSpec(memory_space=pltpu.SMEM)] + [vmem] * 6 + [hbm] * 2,
            out_specs=vmem,
            scratch_shapes=[
                V((3, D, C), bf),
                V((C, D), bf),
                V((M, 2, Z, R, D), bf),
                V((M, J, 2, Z, R, CK), bf),
                V((M, J, 2, Z, R, CK), bf),
                V((M, J, Z, R, CK), bf),
                V((M, J, Z - 1, R, CK), bf),
                V((M, J, R, CK), bf),
                V((M, R, D), f32),
                V((M, L, C), f32),
                V((L, C), f32),
                V((3, L, C), bf),
                V((2, C // HD, L, L), f32),
                V((2, L, C), f32),
                V((L, LANE), f32),
                V((M, R, LANE), f32),
                V((R, LANE), f32),
                V((M, R, LANE), f32),
                V((M, T, R, LANE), f32),
                dma((KX,)),
                dma((J,)),
                dma((M, KX, Z - 1)),
                dma((M,)),
                dma((M,)),
                dma((M, KX, Z - 1)),
                dma((M, KX, Z - 1)),
                dma((M, KX)),
                dma((M, KX)),
                dma((M, J)),
                dma((M, J)),
                dma((M, J, Z - 1)),
                dma((M, J, Z - 1)),
                dma((M, J)),
                dma((M, J)),
                dma((M, J)),
                dma((M, J)),
                dma((M, J, Z - 1)),
                dma((M, J, Z - 1)),
                dma((M, T)),
                dma((M,)),
            ],
            compiler_params=pltpu.CompilerParams(
                collective_id=0, has_side_effects=True, vmem_limit_bytes=62 * 1024 * 1024
            ),
        )(
            layout, cotangent, inputs, norm_gain, queries[0], keys[0], values[0],
            qkv_weight, out_weight,
        )
        return result[None]

    in_specs = (
        P(None, "tensor", None),
        P("pipe", None, "tensor", None),
        P("pipe", None),
        P("pipe", None, None, "tensor"),
        P("pipe", None, None, "tensor"),
        P("pipe", None, None, "tensor"),
        P("pipe", None, None, "tensor"),
        P("pipe", "tensor", None),
        P(),
    )
    out_specs = P("pipe", None, "tensor", None)
    return jax.shard_map(shards, mesh=mesh, in_specs=in_specs, out_specs=out_specs, check_vma=False)
```

```python
import functools
import math

import jax
import jax.numpy as jnp
from jax import lax
from jax.experimental import pallas as pl
from jax.experimental.pallas import tpu as pltpu
from jax.sharding import PartitionSpec as P

HD = 128
LANE = 128
MESH = pl.DeviceIdType.MESH
NT = (((1,), (1,)), ((), ()))
TN = (((0,), (0,)), ((), ()))
NN = (((1,), (0,)), ((), ()))


def mm(a, b, dims):
    return lax.dot_general(a, b, dims, preferred_element_type=jnp.float32)


def combos(dists):
    sets = [()]
    for d in dists:
        sets = sets + [s + (d,) for s in sets]
    return sets


def body(
    sizes,
    layout, cot, xs, gain, qs, ks, vs, wqkv_hbm, wout_hbm,
    out,
    wqkv, wout, xfull, full, part, sibs, zgot, gout, keep, ymat, acc,
    grads, probs_keep, att_keep, coef, factor, dacc, dsend, coefin,
    wout_sem, wqkv_sem, ln_s, xh_s, xh_r, xa_s, xa_r, xs_s, xs_r,
    hop_s, hop_r, g_s, g_r, sg_s, sg_r, rb_s, rb_r, rz_s, rz_r, ci_s, ci_r,
):
    S, T, M, R, D, C, L, J, KX, KA, DIRECT, SKEW = sizes
    Z = T // 2
    CK = D // J
    XK = D // KX
    f32 = jnp.float32
    bf = jnp.bfloat16
    s = lax.axis_index("pipe")
    t = lax.axis_index("tensor")
    z = t // 2
    c = t % 2
    sib = z * 2 + (1 - c)
    scale = 1.0 / math.sqrt(HD)
    last = s == S - 1

    dists = []
    d = Z // 2
    while d >= 1:
        dists.append(d)
        d //= 2
    moves = []
    for i, d in enumerate(dists):
        held = combos(dists[:i])
        moves.append((d, [(len(held) - 1 + n, h) for n, h in enumerate(held)]))
    halves = []
    count = 0
    up = dists[::-1]
    for i, d in enumerate(up):
        held = combos(up[i + 1 :])
        halves.append((d, [(count + n, h) for n, h in enumerate(held)]))
        count += len(held)
    spans = [(n, (d,) + held) for d, pieces in moves for n, held in pieces]
    if DIRECT:
        gmoves = [[(n, ds, ()) for n, ds in spans]]
    else:
        gmoves = [[(n, (d,), held) for n, held in pieces] for d, pieces in moves]

    def flip(v, ds):
        for d in ds:
            v = v + d - 2 * d * ((v // d) % 2)
        return v

    def jcols(j):
        return pl.ds(pl.multiple_of(j * CK, CK), CK)

    def xcols(k):
        return pl.ds(pl.multiple_of(k * XK, XK), XK)

    def remote(src, dst, ss, rs, device):
        return pltpu.make_async_remote_copy(
            src_ref=src, dst_ref=dst, send_sem=ss, recv_sem=rs,
            device_id=device, device_id_type=MESH,
        )

    def loop(n, fn):
        def step(i, carry):
            fn(i)
            return carry
        lax.fori_loop(0, n, step, 0)

    def wout_copy(k):
        return pltpu.make_async_copy(wout_hbm.at[0, :, xcols(k)], wout.at[:, xcols(k)], wout_sem.at[k])

    def wqkv_copy(j):
        return pltpu.make_async_copy(
            wqkv_hbm.at[0, :, jcols(j), :], wqkv.at[:, jcols(j), :], wqkv_sem.at[j]
        )

    def xhop(m, section):
        return remote(xs.at[0, m], xfull.at[m, c, z], xh_s.at[m], xh_r.at[m], (section, t))

    def xmove(m, k, d, n, held):
        ref = xfull.at[m, c, flip(z, held), :, xcols(k)]
        return remote(ref, ref, xa_s.at[m, k, n], xa_r.at[m, k, n], (s, flip(z, (d,)) * 2 + c))

    def xmove_in(m, k, d, n, held):
        ref = xfull.at[m, c, flip(flip(z, (d,)), held), :, xcols(k)]
        return remote(ref, ref, xa_s.at[m, k, n], xa_r.at[m, k, n], (s, flip(z, (d,)) * 2 + c))

    def lend(m, k, n, ds):
        return remote(
            cot.at[m, :, xcols(k)], xfull.at[m, c, z, :, xcols(k)],
            ln_s.at[m, k, n], xa_r.at[m, k, n], (S - 1, flip(z, ds) * 2 + c),
        )

    def lent(m, k):
        return last & ((m > 0) | (k >= KA))

    def lends(m, k):
        if m > 0:
            return S - 3
        return S - 2 - k % 2

    def xsib(m, k):
        ref = xfull.at[m, c, :, :, xcols(k)]
        return remote(ref, ref, xs_s.at[m, k], xs_r.at[m, k], (s, sib))

    def xsib_in(m, k):
        ref = xfull.at[m, 1 - c, :, :, xcols(k)]
        return remote(ref, ref, xs_s.at[m, k], xs_r.at[m, k], (s, sib))

    def hop(u, j, section):
        return remote(
            gout.at[u, j], full.at[u, j, c, z], hop_s.at[u, j], hop_r.at[u, j], (section, t)
        )

    def gmove(u, j, n, ds, held):
        ref = full.at[u, j, c, flip(z, held)]
        return remote(ref, ref, g_s.at[u, j, n], g_r.at[u, j, n], (s, flip(z, ds) * 2 + c))

    def gmove_in(u, j, n, ds, held):
        ref = full.at[u, j, c, flip(flip(z, ds), held)]
        return remote(ref, ref, g_s.at[u, j, n], g_r.at[u, j, n], (s, flip(z, ds) * 2 + c))

    def sg_out(u, j):
        ref = full.at[u, j, c]
        return remote(ref, ref, sg_s.at[u, j], sg_r.at[u, j], (s, sib))

    def sg_in(u, j):
        ref = full.at[u, j, 1 - c]
        return remote(ref, ref, sg_s.at[u, j], sg_r.at[u, j], (s, sib))

    def rb(u, j):
        return remote(part.at[u, j, 1 - c], sibs.at[u, j], rb_s.at[u, j], rb_r.at[u, j], (s, sib))

    def rz(u, j, d, n, held):
        q = flip(z, (d,))
        return remote(
            part.at[u, j, c, flip(q, held)], zgot.at[u, j, n],
            rz_s.at[u, j, n], rz_r.at[u, j, n], (s, q * 2 + c),
        )

    def ci_out(u, o, section):
        return remote(dsend.at[u], coefin.at[u, t], ci_s.at[u, o], ci_r.at[u], (section, o))

    def ci_in(u):
        return remote(coefin.at[u], coefin.at[u], ci_s.at[u, 0], ci_r.at[u], (s, sib))

    barrier = pltpu.get_barrier_semaphore()
    for dt in range(1, T):
        pl.semaphore_signal(barrier, inc=1, device_id=(s, lax.rem(t + dt, T)), device_id_type=MESH)

    @pl.when(s > 0)
    def _():
        for o in range(T):
            pl.semaphore_signal(barrier, inc=1, device_id=(s - 1, o), device_id_type=MESH)

    @pl.when(s < S - 1)
    def _():
        for o in range(T):
            pl.semaphore_signal(barrier, inc=1, device_id=(s + 1, o), device_id_type=MESH)

    @pl.when(last)
    def _():
        for o in range(T):
            pl.semaphore_signal(barrier, inc=1, device_id=(S - 3, o), device_id_type=MESH)

    loop(KX, lambda k: wout_copy(k).start())
    loop(J, lambda j: wqkv_copy(j).start())

    @pl.when(last)
    def _():
        for m in range(M):
            xfull[m, c, z] = cot[m]

    ends = jnp.where(s == 0, 1, 0) + jnp.where(s == S - 1, 1, 0)
    pl.semaphore_wait(barrier, T - 1 + T * (2 - ends) + jnp.where(s == S - 3, T, 0))

    def move_start(m, i):
        d, pieces = moves[i]

        def one(k):
            @pl.when(~lent(m, k))
            def _():
                if i > 0:
                    before, arrived = moves[i - 1]
                    for n, held in arrived:
                        xmove_in(m, k, before, n, held).wait_recv()
                for n, held in pieces:
                    xmove(m, k, d, n, held).start()

        loop(KX, one)

    def move_end(m):
        before, arrived = moves[-1]

        def one(k):
            for n, held in arrived:
                xmove_in(m, k, before, n, held).wait_recv()

            @pl.when(lent(m, k))
            def _():
                for d, pieces in moves[:-1]:
                    for n, held in pieces:
                        xmove_in(m, k, d, n, held).wait_recv()

            xsib(m, k).start()

        loop(KX, one)

    def multiply(m):
        ymat[m] = jnp.zeros((L, C), f32)

        def one(k):
            @pl.when(m == 0)
            def _():
                wout_copy(k).wait()

            xsib_in(m, k).wait_recv()
            rows = jnp.concatenate([xfull[m, o % 2, o // 2, :, xcols(k)] for o in range(T)], axis=0)
            ymat[m] += mm(rows, wout[:, xcols(k)], NT)

        loop(KX, one)

    def lending(fn, units):
        for m in units:
            for k in range(KX):
                if m > 0 or k >= KA:
                    @pl.when(s == lends(m, k))
                    def _():
                        for n, ds in spans:
                            fn(m, k, n, ds)

    @pl.when(last)
    def _():
        move_start(0, 0)

    lending(lambda m, k, n, ds: lend(m, k, n, ds).start(), range(0, 1))

    @pl.when(s > 0)
    def _():
        for m in range(M):
            xhop(m, s - 1).start()

    lending(lambda m, k, n, ds: lend(m, k, n, ds).wait_send(), range(0, 1))
    lending(lambda m, k, n, ds: lend(m, k, n, ds).start(), range(1, M))

    for m in range(M):
        def square(k, carry):
            x = xs[0, m, :, xcols(k)].astype(f32)
            return carry + jnp.sum(x * x, axis=1, keepdims=True)

        squares = lax.fori_loop(0, KX, square, jnp.zeros((R, 1), f32))
        factor[m] = jnp.broadcast_to(lax.rsqrt(squares / D + 1e-05), (R, LANE))

    @pl.when(last)
    def _():
        for i in range(1, len(moves)):
            move_start(0, i)
        move_end(0)
        multiply(0)

    @pl.when(s < S - 1)
    def _():
        for m in range(M):
            xhop(m, s).wait_recv()
            move_start(m, 0)
        for i in range(1, len(moves)):
            for m in range(M):
                move_start(m, i)
        move_end(0)
        multiply(0)

    @pl.when(s < S - 2)
    def _():
        for m in range(1, M):
            move_end(m)
            multiply(m)

    def prepare(u):
        nb = layout.shape[1]
        bl = L // nb
        kb = lax.broadcasted_iota(jnp.int32, (bl, L), 1) // bl
        strips = []
        for b in range(nb):
            strip = kb == layout[u, b, 0]
            for e in range(1, layout.shape[2]):
                strip = strip | (kb == layout[u, b, e])
            strips.append(jnp.where(strip, 1.0, 0.0))
        listed = jnp.concatenate(strips, axis=0)
        row = lax.broadcasted_iota(jnp.int32, (L, L), 0)
        col = lax.broadcasted_iota(jnp.int32, (L, L), 1)
        allowed = (listed > 0.5) & (col <= row)
        for h in range(C // HD):
            hc = slice(h * HD, (h + 1) * HD)
            scores = jnp.where(allowed, mm(qs[u, :, hc], ks[u, :, hc], NT) * scale, -1e30)
            expo = jnp.exp(scores - jnp.max(scores, axis=1, keepdims=True))
            probs = expo / jnp.sum(expo, axis=1, keepdims=True)
            probs_keep[u % 2, h] = probs
            att_keep[u % 2, :, hc] = mm(probs.astype(bf), vs[u, :, hc], NN)

    def attend(u):
        @pl.when(last)
        def _():
            coef[...] = jnp.full((L, LANE), -1.0, f32)

        @pl.when(s < S - 1)
        def _():
            ci_in(u).wait_recv()
            coef[...] = jnp.concatenate([coefin[u, o] for o in range(T)], axis=0)

        for h in range(C // HD):
            hc = slice(h * HD, (h + 1) * HD)
            query = qs[u, :, hc]
            key = ks[u, :, hc]
            value = vs[u, :, hc]
            go = (acc[:, hc] - coef[...] * ymat[u, :, hc]).astype(bf)
            probs = probs_keep[u % 2, h]
            delta = jnp.sum(att_keep[u % 2, :, hc] * go.astype(f32), axis=1, keepdims=True)
            dprob = mm(go, value, NT)
            dscore = (probs * (dprob - delta)).astype(bf)
            grads[0, :, hc] = (mm(dscore, key, NN) * scale).astype(bf)
            grads[1, :, hc] = (mm(dscore, query, TN) * scale).astype(bf)
            grads[2, :, hc] = mm(probs.astype(bf), go, TN).astype(bf)
        dacc[...] = jnp.zeros_like(dacc)

    def produce(u, j):
        @pl.when(u == 0)
        def _():
            wqkv_copy(j).wait()

        cols = jcols(j)
        value = mm(grads[0], wqkv[0, cols, :], NT)
        value = value + mm(grads[1], wqkv[1, cols, :], NT)
        value = value + mm(grads[2], wqkv[2, cols, :], NT)
        value = value.astype(bf)
        for o in range(T):
            part[u, j, o % 2, o // 2] = value[o * R : (o + 1) * R]
        rb(u, j).start()

    def combine(u, j, i):
        if i == 0:
            rb(u, j).wait_recv()
            part[u, j, c] = (part[u, j, c].astype(f32) + sibs[u, j].astype(f32)).astype(bf)
        else:
            before, arrived = halves[i - 1]
            for n, held in arrived:
                rz(u, j, before, n, held).wait_recv()
            for n, held in arrived:
                if held:
                    at = flip(z, held)
                    total = part[u, j, c, at].astype(f32) + zgot[u, j, n].astype(f32)
                    part[u, j, c, at] = total.astype(bf)
        d, pieces = halves[i]
        for n, held in pieces:
            rz(u, j, d, n, held).start()

    def finish(u, j):
        before, arrived = halves[-1]
        for n, held in arrived:
            rz(u, j, before, n, held).wait_recv()
        cols = jcols(j)
        total = part[u, j, c, z].astype(f32)
        for d, pieces in halves:
            total = total + zgot[u, j, pieces[0][0]].astype(f32)
        scaled = total * gain[:, cols]
        mine = coef[pl.ds(pl.multiple_of(t * R, R), R), :][:, 0:1]
        above = xfull[u, c, z, :, cols].astype(f32)
        came = jnp.where(last, 0.0, full[u, j, c, z].astype(f32))
        value = came - mine * above + factor[u][:, 0:1] * scaled
        keep[u, :, cols] = value

        @pl.when(s > 0)
        def _():
            gout[u, j] = value.astype(bf)
            hop(u, j, s - 1).start()

        product = scaled * xs[0, u, :, cols].astype(f32)
        sums = product[:, 0:LANE]
        for i in range(1, CK // LANE):
            sums = sums + product[:, i * LANE : (i + 1) * LANE]
        dacc[...] += sums

    def settle(u):
        r = factor[u]
        dots = jnp.sum(dacc[...], axis=1, keepdims=True)
        dsend[u] = r * r * dots * (1.0 / D)

        @pl.when(s > 0)
        def _():
            for o in range(T):
                ci_out(u, o, s - 1).start()

    def give(u):
        cc = dsend[u][:, 0:1]

        def one(j):
            cols = jcols(j)
            out[u, :, cols] = (keep[u, :, cols] - cc * xs[0, u, :, cols].astype(f32)).astype(bf)

        loop(J, one)

    def spread(u, j, i):
        if i == 0:
            hop(u, j, s).wait_recv()
        else:
            for move in gmoves[i - 1]:
                gmove_in(u, j, *move).wait_recv()
        if i < len(gmoves):
            for move in gmoves[i]:
                gmove(u, j, *move).start()
        else:
            sg_out(u, j).start()

    def project(u, j):
        sg_in(u, j).wait_recv()
        rows = jnp.concatenate([full[u, j, o % 2, o // 2] for o in range(T)], axis=0)
        acc[...] += mm(rows, wout[:, jcols(j)], NT)

    P1, PD, QA, QB, QD = SKEW
    PE = P1 + PD * len(halves)
    Q0 = jnp.where(s == S - 2, QA, QB)
    QE = Q0 + QD * (len(gmoves) + 1)
    steps = J + max(PE, max(QA, QB) + QD * (len(gmoves) + 1))

    def merged(n):
        u = n - 1
        mine = u >= 0
        more = u + 1 < M

        @pl.when((s >= S - 2) & (u > 0))
        def _():
            multiply(u)

        @pl.when(mine)
        def _():
            attend(u)

        acc[...] = jnp.zeros_like(acc)

        def step(i):
            def on(skew):
                return (i >= skew) & (i < J + skew)

            @pl.when(mine)
            def _():
                @pl.when(i < J)
                def _():
                    produce(u, i)

                for k in range(len(halves)):
                    @pl.when(on(P1 + PD * k))
                    def _():
                        combine(u, i - (P1 + PD * k), k)

                @pl.when(on(PE))
                def _():
                    finish(u, i - PE)

                @pl.when(i == J + PE - 1)
                def _():
                    settle(u)
                    give(u)

            @pl.when(more & (i == jnp.where(mine, J, 0)))
            def _():
                prepare(u + 1)

            @pl.when(more & (s < S - 1))
            def _():
                for k in range(len(gmoves) + 1):
                    @pl.when(on(Q0 + QD * k))
                    def _():
                        spread(u + 1, i - (Q0 + QD * k), k)

                @pl.when(on(QE))
                def _():
                    project(u + 1, i - QE)

        loop(steps, step)

        @pl.when((s >= S - 2) & mine & more)
        def _():
            move_end(u + 1)

    loop(M + 1, merged)

    lending(lambda m, k, n, ds: lend(m, k, n, ds).wait_send(), range(1, M))

    @pl.when(s > 0)
    def _():
        for m in range(M):
            xhop(m, s - 1).wait_send()

    def drain(m):
        def drain_k(k):
            @pl.when(~lent(m, k))
            def _():
                for d, pieces in moves:
                    for n, held in pieces:
                        xmove(m, k, d, n, held).wait_send()

            xsib(m, k).wait_send()

        loop(KX, drain_k)

        def drain_j(j):
            rb(m, j).wait_send()
            for d, pieces in halves:
                for n, held in pieces:
                    rz(m, j, d, n, held).wait_send()

            @pl.when(s < S - 1)
            def _():
                for moved in gmoves:
                    for move in moved:
                        gmove(m, j, *move).wait_send()
                sg_out(m, j).wait_send()

            @pl.when(s > 0)
            def _():
                hop(m, j, s - 1).wait_send()

        loop(J, drain_j)

        @pl.when(s > 0)
        def _():
            for o in range(T):
                ci_out(m, o, s - 1).wait_send()

    loop(M, drain)


def solution(mesh):
    S = mesh.shape["pipe"]
    T = mesh.shape["tensor"]

    def shards(cotangent, inputs, norm_gain, queries, keys, values, qkv_weight, out_weight, layout):
        M, R, D = cotangent.shape
        C = queries.shape[3]
        L = queries.shape[2]
        Z = T // 2
        J = 8
        KX = 4
        KA = 2
        DIRECT = False
        SKEW = (1, 2, 9, 12, 2)
        CK = D // J
        sizes = (S, T, M, R, D, C, L, J, KX, KA, DIRECT, SKEW)
        vmem = pl.BlockSpec(memory_space=pltpu.VMEM)
        hbm = pl.BlockSpec(memory_space=pl.ANY)
        bf = jnp.bfloat16
        f32 = jnp.float32
        dma = pltpu.SemaphoreType.DMA
        V = pltpu.VMEM
        result = pl.pallas_call(
            functools.partial(body, sizes),
            out_shape=jax.ShapeDtypeStruct((M, R, D), bf),
            in_specs=[pl.BlockSpec(memory_space=pltpu.SMEM)] + [vmem] * 6 + [hbm] * 2,
            out_specs=vmem,
            scratch_shapes=[
                V((3, D, C), bf),
                V((C, D), bf),
                V((M, 2, Z, R, D), bf),
                V((M, J, 2, Z, R, CK), bf),
                V((M, J, 2, Z, R, CK), bf),
                V((M, J, Z, R, CK), bf),
                V((M, J, Z - 1, R, CK), bf),
                V((M, J, R, CK), bf),
                V((M, R, D), f32),
                V((M, L, C), f32),
                V((L, C), f32),
                V((3, L, C), bf),
                V((2, C // HD, L, L), f32),
                V((2, L, C), f32),
                V((L, LANE), f32),
                V((M, R, LANE), f32),
                V((R, LANE), f32),
                V((M, R, LANE), f32),
                V((M, T, R, LANE), f32),
                dma((KX,)),
                dma((J,)),
                dma((M, KX, Z - 1)),
                dma((M,)),
                dma((M,)),
                dma((M, KX, Z - 1)),
                dma((M, KX, Z - 1)),
                dma((M, KX)),
                dma((M, KX)),
                dma((M, J)),
                dma((M, J)),
                dma((M, J, Z - 1)),
                dma((M, J, Z - 1)),
                dma((M, J)),
                dma((M, J)),
                dma((M, J)),
                dma((M, J)),
                dma((M, J, Z - 1)),
                dma((M, J, Z - 1)),
                dma((M, T)),
                dma((M,)),
            ],
            compiler_params=pltpu.CompilerParams(
                collective_id=0, has_side_effects=True, vmem_limit_bytes=62 * 1024 * 1024
            ),
        )(
            layout, cotangent, inputs, norm_gain, queries[0], keys[0], values[0],
            qkv_weight, out_weight,
        )
        return result[None]

    in_specs = (
        P(None, "tensor", None),
        P("pipe", None, "tensor", None),
        P("pipe", None),
        P("pipe", None, None, "tensor"),
        P("pipe", None, None, "tensor"),
        P("pipe", None, None, "tensor"),
        P("pipe", None, None, "tensor"),
        P("pipe", "tensor", None),
        P(),
    )
    out_specs = P("pipe", None, "tensor", None)
    return jax.shard_map(shards, mesh=mesh, in_specs=in_specs, out_specs=out_specs, check_vma=False)
```

```python
import functools
import math

import jax
import jax.numpy as jnp
from jax import lax
from jax.experimental import pallas as pl
from jax.experimental.pallas import tpu as pltpu
from jax.sharding import PartitionSpec as P

HD = 128
LANE = 128
MESH = pl.DeviceIdType.MESH
NT = (((1,), (1,)), ((), ()))
TN = (((0,), (0,)), ((), ()))
NN = (((1,), (0,)), ((), ()))


def mm(a, b, dims):
    return lax.dot_general(a, b, dims, preferred_element_type=jnp.float32)


def combos(dists):
    sets = [()]
    for d in dists:
        sets = sets + [s + (d,) for s in sets]
    return sets


def body(
    sizes,
    layout, cot, xs, gain, qs, ks, vs, wqkv_hbm, wout_hbm,
    out,
    wqkv, wout, xfull, full, part, sibs, zgot, gout, keep, ymat, acc,
    grads, probs_keep, att_keep, coef, factor, dacc, dsend, coefin,
    wout_sem, wqkv_sem, ln_s, xh_s, xh_r, xa_s, xa_r, xs_s, xs_r,
    hop_s, hop_r, g_s, g_r, sg_s, sg_r, rb_s, rb_r, rz_s, rz_r, ci_s, ci_r,
):
    S, T, M, R, D, C, L, J, KX, KA, DIRECT, SKEW = sizes
    Z = T // 2
    CK = D // J
    XK = D // KX
    f32 = jnp.float32
    bf = jnp.bfloat16
    s = lax.axis_index("pipe")
    t = lax.axis_index("tensor")
    z = t // 2
    c = t % 2
    sib = z * 2 + (1 - c)
    scale = 1.0 / math.sqrt(HD)
    last = s == S - 1

    dists = []
    d = Z // 2
    while d >= 1:
        dists.append(d)
        d //= 2
    moves = []
    for i, d in enumerate(dists):
        held = combos(dists[:i])
        moves.append((d, [(len(held) - 1 + n, h) for n, h in enumerate(held)]))
    halves = []
    count = 0
    up = dists[::-1]
    for i, d in enumerate(up):
        held = combos(up[i + 1 :])
        halves.append((d, [(count + n, h) for n, h in enumerate(held)]))
        count += len(held)
    spans = [(n, (d,) + held) for d, pieces in moves for n, held in pieces]
    if DIRECT:
        gmoves = [[(n, ds, ()) for n, ds in spans]]
    else:
        gmoves = [
            [(n, (d,), held) for d, pieces in moves for n, held in pieces if len(held) == i]
            for i in range(len(moves))
        ]

    def flip(v, ds):
        for d in ds:
            v = v + d - 2 * d * ((v // d) % 2)
        return v

    def jcols(j):
        return pl.ds(pl.multiple_of(j * CK, CK), CK)

    def xcols(k):
        return pl.ds(pl.multiple_of(k * XK, XK), XK)

    def remote(src, dst, ss, rs, device):
        return pltpu.make_async_remote_copy(
            src_ref=src, dst_ref=dst, send_sem=ss, recv_sem=rs,
            device_id=device, device_id_type=MESH,
        )

    def loop(n, fn):
        def step(i, carry):
            fn(i)
            return carry
        lax.fori_loop(0, n, step, 0)

    def wout_copy(k):
        return pltpu.make_async_copy(wout_hbm.at[0, :, xcols(k)], wout.at[:, xcols(k)], wout_sem.at[k])

    def wqkv_copy(j):
        return pltpu.make_async_copy(
            wqkv_hbm.at[0, :, jcols(j), :], wqkv.at[:, jcols(j), :], wqkv_sem.at[j]
        )

    def xhop(m, section):
        return remote(xs.at[0, m], xfull.at[m, c, z], xh_s.at[m], xh_r.at[m], (section, t))

    def xmove(m, k, d, n, held):
        ref = xfull.at[m, c, flip(z, held), :, xcols(k)]
        return remote(ref, ref, xa_s.at[m, k, n], xa_r.at[m, k, n], (s, flip(z, (d,)) * 2 + c))

    def xmove_in(m, k, d, n, held):
        ref = xfull.at[m, c, flip(flip(z, (d,)), held), :, xcols(k)]
        return remote(ref, ref, xa_s.at[m, k, n], xa_r.at[m, k, n], (s, flip(z, (d,)) * 2 + c))

    def lend(m, k, n, ds):
        return remote(
            cot.at[m, :, xcols(k)], xfull.at[m, c, z, :, xcols(k)],
            ln_s.at[m, k, n], xa_r.at[m, k, n], (S - 1, flip(z, ds) * 2 + c),
        )

    def lent(m, k):
        return last & ((m > 0) | (k >= KA))

    def lends(m, k):
        if m > 0:
            return S - 3
        return S - 2 - k % 2

    def xsib(m, k):
        ref = xfull.at[m, c, :, :, xcols(k)]
        return remote(ref, ref, xs_s.at[m, k], xs_r.at[m, k], (s, sib))

    def xsib_in(m, k):
        ref = xfull.at[m, 1 - c, :, :, xcols(k)]
        return remote(ref, ref, xs_s.at[m, k], xs_r.at[m, k], (s, sib))

    def hop(u, j, section):
        return remote(
            gout.at[u, j], full.at[u, j, c, z], hop_s.at[u, j], hop_r.at[u, j], (section, t)
        )

    def gmove(u, j, n, ds, held):
        ref = full.at[u, j, c, flip(z, held)]
        return remote(ref, ref, g_s.at[u, j, n], g_r.at[u, j, n], (s, flip(z, ds) * 2 + c))

    def gmove_in(u, j, n, ds, held):
        ref = full.at[u, j, c, flip(flip(z, ds), held)]
        return remote(ref, ref, g_s.at[u, j, n], g_r.at[u, j, n], (s, flip(z, ds) * 2 + c))

    def sg_out(u, j):
        ref = full.at[u, j, c]
        return remote(ref, ref, sg_s.at[u, j], sg_r.at[u, j], (s, sib))

    def sg_in(u, j):
        ref = full.at[u, j, 1 - c]
        return remote(ref, ref, sg_s.at[u, j], sg_r.at[u, j], (s, sib))

    def rb(u, j):
        return remote(part.at[u, j, 1 - c], sibs.at[u, j], rb_s.at[u, j], rb_r.at[u, j], (s, sib))

    def rz(u, j, d, n, held):
        q = flip(z, (d,))
        return remote(
            part.at[u, j, c, flip(q, held)], zgot.at[u, j, n],
            rz_s.at[u, j, n], rz_r.at[u, j, n], (s, q * 2 + c),
        )

    def ci_out(u, o, section):
        return remote(dsend.at[u], coefin.at[u, t], ci_s.at[u, o], ci_r.at[u], (section, o))

    def ci_in(u):
        return remote(coefin.at[u], coefin.at[u], ci_s.at[u, 0], ci_r.at[u], (s, sib))

    barrier = pltpu.get_barrier_semaphore()
    for dt in range(1, T):
        pl.semaphore_signal(barrier, inc=1, device_id=(s, lax.rem(t + dt, T)), device_id_type=MESH)

    @pl.when(s > 0)
    def _():
        for o in range(T):
            pl.semaphore_signal(barrier, inc=1, device_id=(s - 1, o), device_id_type=MESH)

    @pl.when(s < S - 1)
    def _():
        for o in range(T):
            pl.semaphore_signal(barrier, inc=1, device_id=(s + 1, o), device_id_type=MESH)

    @pl.when(last)
    def _():
        for o in range(T):
            pl.semaphore_signal(barrier, inc=1, device_id=(S - 3, o), device_id_type=MESH)

    loop(KX, lambda k: wout_copy(k).start())
    loop(J, lambda j: wqkv_copy(j).start())

    @pl.when(last)
    def _():
        for m in range(M):
            xfull[m, c, z] = cot[m]

    ends = jnp.where(s == 0, 1, 0) + jnp.where(s == S - 1, 1, 0)
    pl.semaphore_wait(barrier, T - 1 + T * (2 - ends) + jnp.where(s == S - 3, T, 0))

    def move_start(m, i):
        d, pieces = moves[i]

        def one(k):
            @pl.when(~lent(m, k))
            def _():
                if i > 0:
                    before, arrived = moves[i - 1]
                    for n, held in arrived:
                        xmove_in(m, k, before, n, held).wait_recv()
                for n, held in pieces:
                    xmove(m, k, d, n, held).start()

        loop(KX, one)

    def move_end(m):
        before, arrived = moves[-1]

        def one(k):
            for n, held in arrived:
                xmove_in(m, k, before, n, held).wait_recv()

            @pl.when(lent(m, k))
            def _():
                for d, pieces in moves[:-1]:
                    for n, held in pieces:
                        xmove_in(m, k, d, n, held).wait_recv()

            xsib(m, k).start()

        loop(KX, one)

    def multiply(m):
        ymat[m] = jnp.zeros((L, C), f32)

        def one(k):
            @pl.when(m == 0)
            def _():
                wout_copy(k).wait()

            xsib_in(m, k).wait_recv()
            rows = jnp.concatenate([xfull[m, o % 2, o // 2, :, xcols(k)] for o in range(T)], axis=0)
            ymat[m] += mm(rows, wout[:, xcols(k)], NT)

        loop(KX, one)

    def lending(fn, units):
        for m in units:
            for k in range(KX):
                if m > 0 or k >= KA:
                    @pl.when(s == lends(m, k))
                    def _():
                        for n, ds in spans:
                            fn(m, k, n, ds)

    @pl.when(last)
    def _():
        move_start(0, 0)

    lending(lambda m, k, n, ds: lend(m, k, n, ds).start(), range(0, 1))

    @pl.when(s > 0)
    def _():
        for m in range(M):
            xhop(m, s - 1).start()

    lending(lambda m, k, n, ds: lend(m, k, n, ds).wait_send(), range(0, 1))
    lending(lambda m, k, n, ds: lend(m, k, n, ds).start(), range(1, M))

    def prepare(u):
        nb = layout.shape[1]
        bl = L // nb
        kb = lax.broadcasted_iota(jnp.int32, (bl, L), 1) // bl
        strips = []
        for b in range(nb):
            strip = kb == layout[u, b, 0]
            for e in range(1, layout.shape[2]):
                strip = strip | (kb == layout[u, b, e])
            strips.append(jnp.where(strip, 1.0, 0.0))
        listed = jnp.concatenate(strips, axis=0)
        row = lax.broadcasted_iota(jnp.int32, (L, L), 0)
        col = lax.broadcasted_iota(jnp.int32, (L, L), 1)
        allowed = (listed > 0.5) & (col <= row)
        for h in range(C // HD):
            hc = slice(h * HD, (h + 1) * HD)
            scores = jnp.where(allowed, mm(qs[u, :, hc], ks[u, :, hc], NT) * scale, -1e30)
            expo = jnp.exp(scores - jnp.max(scores, axis=1, keepdims=True))
            probs = expo / jnp.sum(expo, axis=1, keepdims=True)
            probs_keep[u, h] = probs
            att_keep[u, :, hc] = mm(probs.astype(bf), vs[u, :, hc], NN)

    for m in range(M):
        def square(k, carry):
            x = xs[0, m, :, xcols(k)].astype(f32)
            return carry + jnp.sum(x * x, axis=1, keepdims=True)

        squares = lax.fori_loop(0, KX, square, jnp.zeros((R, 1), f32))
        factor[m] = jnp.broadcast_to(lax.rsqrt(squares / D + 1e-05), (R, LANE))

    prepare(0)

    @pl.when(last)
    def _():
        for i in range(1, len(moves)):
            move_start(0, i)

    for m in range(1, M):
        prepare(m)

    @pl.when(last)
    def _():
        move_end(0)
        multiply(0)

    @pl.when(s < S - 1)
    def _():
        for m in range(M):
            xhop(m, s).wait_recv()
            move_start(m, 0)
        for i in range(1, len(moves)):
            for m in range(M):
                move_start(m, i)
        move_end(0)
        multiply(0)

    @pl.when(s < S - 2)
    def _():
        for m in range(1, M):
            move_end(m)
            multiply(m)

    def attend(u):
        @pl.when(last)
        def _():
            coef[...] = jnp.full((L, LANE), -1.0, f32)

        @pl.when(s < S - 1)
        def _():
            ci_in(u).wait_recv()
            coef[...] = jnp.concatenate([coefin[u, o] for o in range(T)], axis=0)

        for h in range(C // HD):
            hc = slice(h * HD, (h + 1) * HD)
            query = qs[u, :, hc]
            key = ks[u, :, hc]
            value = vs[u, :, hc]
            go = (acc[:, hc] - coef[...] * ymat[u, :, hc]).astype(bf)
            probs = probs_keep[u, h]
            delta = jnp.sum(att_keep[u, :, hc] * go.astype(f32), axis=1, keepdims=True)
            dprob = mm(go, value, NT)
            dscore = (probs * (dprob - delta)).astype(bf)
            grads[0, :, hc] = (mm(dscore, key, NN) * scale).astype(bf)
            grads[1, :, hc] = (mm(dscore, query, TN) * scale).astype(bf)
            grads[2, :, hc] = mm(probs.astype(bf), go, TN).astype(bf)
        dacc[...] = jnp.zeros_like(dacc)

    def produce(u, j):
        @pl.when(u == 0)
        def _():
            wqkv_copy(j).wait()

        cols = jcols(j)
        value = mm(grads[0], wqkv[0, cols, :], NT)
        value = value + mm(grads[1], wqkv[1, cols, :], NT)
        value = value + mm(grads[2], wqkv[2, cols, :], NT)
        value = value.astype(bf)
        for o in range(T):
            part[u, j, o % 2, o // 2] = value[o * R : (o + 1) * R]
        rb(u, j).start()

    def combine(u, j, i):
        if i == 0:
            rb(u, j).wait_recv()
            part[u, j, c] = (part[u, j, c].astype(f32) + sibs[u, j].astype(f32)).astype(bf)
        else:
            before, arrived = halves[i - 1]
            for n, held in arrived:
                rz(u, j, before, n, held).wait_recv()
            for n, held in arrived:
                if held:
                    at = flip(z, held)
                    total = part[u, j, c, at].astype(f32) + zgot[u, j, n].astype(f32)
                    part[u, j, c, at] = total.astype(bf)
        d, pieces = halves[i]
        for n, held in pieces:
            rz(u, j, d, n, held).start()

    def finish(u, j):
        before, arrived = halves[-1]
        for n, held in arrived:
            rz(u, j, before, n, held).wait_recv()
        cols = jcols(j)
        total = part[u, j, c, z].astype(f32)
        for d, pieces in halves:
            total = total + zgot[u, j, pieces[0][0]].astype(f32)
        scaled = total * gain[:, cols]
        mine = coef[pl.ds(pl.multiple_of(t * R, R), R), :][:, 0:1]
        above = xfull[u, c, z, :, cols].astype(f32)
        came = jnp.where(last, 0.0, full[u, j, c, z].astype(f32))
        value = came - mine * above + factor[u][:, 0:1] * scaled
        keep[u, :, cols] = value

        @pl.when(s > 0)
        def _():
            gout[u, j] = value.astype(bf)
            hop(u, j, s - 1).start()

        product = scaled * xs[0, u, :, cols].astype(f32)
        sums = product[:, 0:LANE]
        for i in range(1, CK // LANE):
            sums = sums + product[:, i * LANE : (i + 1) * LANE]
        dacc[...] += sums

    def settle(u):
        r = factor[u]
        dots = jnp.sum(dacc[...], axis=1, keepdims=True)
        dsend[u] = r * r * dots * (1.0 / D)

        @pl.when(s > 0)
        def _():
            for o in range(T):
                ci_out(u, o, s - 1).start()

    def give(u):
        cc = dsend[u][:, 0:1]

        def one(j):
            cols = jcols(j)
            out[u, :, cols] = (keep[u, :, cols] - cc * xs[0, u, :, cols].astype(f32)).astype(bf)

        loop(J, one)

    def spread(u, j, i):
        if i == 0:
            hop(u, j, s).wait_recv()
        else:
            for move in gmoves[i - 1]:
                gmove_in(u, j, *move).wait_recv()
        if i < len(gmoves):
            for move in gmoves[i]:
                gmove(u, j, *move).start()
        else:
            sg_out(u, j).start()

    def project(u, j):
        sg_in(u, j).wait_recv()
        rows = jnp.concatenate([full[u, j, o % 2, o // 2] for o in range(T)], axis=0)
        acc[...] += mm(rows, wout[:, jcols(j)], NT)

    P1, PD, QA, QB, QD = SKEW
    PE = P1 + PD * len(halves)
    Q0 = jnp.where(s == S - 2, QA, QB)
    QE = Q0 + QD * (len(gmoves) + 1)
    steps = J + max(PE, max(QA, QB) + QD * (len(gmoves) + 1))

    def merged(n):
        u = n - 1
        mine = u >= 0
        more = u + 1 < M

        @pl.when((s >= S - 2) & (u > 0))
        def _():
            multiply(u)

        @pl.when(mine)
        def _():
            attend(u)

        acc[...] = jnp.zeros_like(acc)

        def step(i):
            def on(skew):
                return (i >= skew) & (i < J + skew)

            @pl.when(mine)
            def _():
                @pl.when(i < J)
                def _():
                    produce(u, i)

                for k in range(len(halves)):
                    @pl.when(on(P1 + PD * k))
                    def _():
                        combine(u, i - (P1 + PD * k), k)

                @pl.when(on(PE))
                def _():
                    finish(u, i - PE)

                @pl.when(i == J + PE - 1)
                def _():
                    settle(u)
                    give(u)

            @pl.when(more & (s < S - 1))
            def _():
                for k in range(len(gmoves) + 1):
                    @pl.when(on(Q0 + QD * k))
                    def _():
                        spread(u + 1, i - (Q0 + QD * k), k)

                @pl.when(on(QE))
                def _():
                    project(u + 1, i - QE)

        loop(steps, step)

        @pl.when((s >= S - 2) & mine & more)
        def _():
            move_end(u + 1)

    loop(M + 1, merged)

    lending(lambda m, k, n, ds: lend(m, k, n, ds).wait_send(), range(1, M))

    @pl.when(s > 0)
    def _():
        for m in range(M):
            xhop(m, s - 1).wait_send()

    def drain(m):
        def drain_k(k):
            @pl.when(~lent(m, k))
            def _():
                for d, pieces in moves:
                    for n, held in pieces:
                        xmove(m, k, d, n, held).wait_send()

            xsib(m, k).wait_send()

        loop(KX, drain_k)

        def drain_j(j):
            rb(m, j).wait_send()
            for d, pieces in halves:
                for n, held in pieces:
                    rz(m, j, d, n, held).wait_send()

            @pl.when(s < S - 1)
            def _():
                for moved in gmoves:
                    for move in moved:
                        gmove(m, j, *move).wait_send()
                sg_out(m, j).wait_send()

            @pl.when(s > 0)
            def _():
                hop(m, j, s - 1).wait_send()

        loop(J, drain_j)

        @pl.when(s > 0)
        def _():
            for o in range(T):
                ci_out(m, o, s - 1).wait_send()

    loop(M, drain)


def solution(mesh):
    S = mesh.shape["pipe"]
    T = mesh.shape["tensor"]

    def shards(cotangent, inputs, norm_gain, queries, keys, values, qkv_weight, out_weight, layout):
        M, R, D = cotangent.shape
        C = queries.shape[3]
        L = queries.shape[2]
        Z = T // 2
        J = 8
        KX = 4
        KA = 2
        DIRECT = False
        SKEW = (1, 2, 9, 12, 2)
        CK = D // J
        sizes = (S, T, M, R, D, C, L, J, KX, KA, DIRECT, SKEW)
        vmem = pl.BlockSpec(memory_space=pltpu.VMEM)
        hbm = pl.BlockSpec(memory_space=pl.ANY)
        bf = jnp.bfloat16
        f32 = jnp.float32
        dma = pltpu.SemaphoreType.DMA
        V = pltpu.VMEM
        result = pl.pallas_call(
            functools.partial(body, sizes),
            out_shape=jax.ShapeDtypeStruct((M, R, D), bf),
            in_specs=[pl.BlockSpec(memory_space=pltpu.SMEM)] + [vmem] * 6 + [hbm] * 2,
            out_specs=vmem,
            scratch_shapes=[
                V((3, D, C), bf),
                V((C, D), bf),
                V((M, 2, Z, R, D), bf),
                V((M, J, 2, Z, R, CK), bf),
                V((M, J, 2, Z, R, CK), bf),
                V((M, J, Z, R, CK), bf),
                V((M, J, Z - 1, R, CK), bf),
                V((M, J, R, CK), bf),
                V((M, R, D), f32),
                V((M, L, C), f32),
                V((L, C), f32),
                V((3, L, C), bf),
                V((M, C // HD, L, L), f32),
                V((M, L, C), f32),
                V((L, LANE), f32),
                V((M, R, LANE), f32),
                V((R, LANE), f32),
                V((M, R, LANE), f32),
                V((M, T, R, LANE), f32),
                dma((KX,)),
                dma((J,)),
                dma((M, KX, Z - 1)),
                dma((M,)),
                dma((M,)),
                dma((M, KX, Z - 1)),
                dma((M, KX, Z - 1)),
                dma((M, KX)),
                dma((M, KX)),
                dma((M, J)),
                dma((M, J)),
                dma((M, J, Z - 1)),
                dma((M, J, Z - 1)),
                dma((M, J)),
                dma((M, J)),
                dma((M, J)),
                dma((M, J)),
                dma((M, J, Z - 1)),
                dma((M, J, Z - 1)),
                dma((M, T)),
                dma((M,)),
            ],
            compiler_params=pltpu.CompilerParams(
                collective_id=0, has_side_effects=True, vmem_limit_bytes=62 * 1024 * 1024
            ),
        )(
            layout, cotangent, inputs, norm_gain, queries[0], keys[0], values[0],
            qkv_weight, out_weight,
        )
        return result[None]

    in_specs = (
        P(None, "tensor", None),
        P("pipe", None, "tensor", None),
        P("pipe", None),
        P("pipe", None, None, "tensor"),
        P("pipe", None, None, "tensor"),
        P("pipe", None, None, "tensor"),
        P("pipe", None, None, "tensor"),
        P("pipe", "tensor", None),
        P(),
    )
    out_specs = P("pipe", None, "tensor", None)
    return jax.shard_map(shards, mesh=mesh, in_specs=in_specs, out_specs=out_specs, check_vma=False)
```

```python
import functools
import math

import jax
import jax.numpy as jnp
from jax import lax
from jax.experimental import pallas as pl
from jax.experimental.pallas import tpu as pltpu
from jax.sharding import PartitionSpec as P

HD = 128
LANE = 128
MESH = pl.DeviceIdType.MESH
NT = (((1,), (1,)), ((), ()))
TN = (((0,), (0,)), ((), ()))
NN = (((1,), (0,)), ((), ()))


def mm(a, b, dims):
    return lax.dot_general(a, b, dims, preferred_element_type=jnp.float32)


def combos(dists):
    sets = [()]
    for d in dists:
        sets = sets + [s + (d,) for s in sets]
    return sets


def body(
    sizes,
    layout, cot, xs, gain, qs, ks, vs, wqkv_hbm, wout_hbm,
    out,
    wqkv, wout, xfull, full, part, sibs, zgot, gout, keep, ymat, acc,
    grads, probs_keep, att_keep, coef, factor, dacc, dsend, coefin,
    wout_sem, wqkv_sem, ln_s, xh_s, xh_r, xa_s, xa_r, xs_s, xs_r,
    hop_s, hop_r, g_s, g_r, sg_s, sg_r, rb_s, rb_r, rz_s, rz_r, ci_s, ci_r,
):
    S, T, M, R, D, C, L, J, KX, KA, DIRECT, SKEW = sizes
    Z = T // 2
    CK = D // J
    XK = D // KX
    f32 = jnp.float32
    bf = jnp.bfloat16
    s = lax.axis_index("pipe")
    t = lax.axis_index("tensor")
    z = t // 2
    c = t % 2
    sib = z * 2 + (1 - c)
    scale = 1.0 / math.sqrt(HD)
    last = s == S - 1

    dists = []
    d = Z // 2
    while d >= 1:
        dists.append(d)
        d //= 2
    moves = []
    for i, d in enumerate(dists):
        held = combos(dists[:i])
        moves.append((d, [(len(held) - 1 + n, h) for n, h in enumerate(held)]))
    halves = []
    count = 0
    up = dists[::-1]
    for i, d in enumerate(up):
        held = combos(up[i + 1 :])
        halves.append((d, [(count + n, h) for n, h in enumerate(held)]))
        count += len(held)
    spans = [(n, (d,) + held) for d, pieces in moves for n, held in pieces]
    if DIRECT:
        gmoves = [[(n, ds, ()) for n, ds in spans]]
    else:
        gmoves = [
            [(n, (d,), held) for d, pieces in moves for n, held in pieces if len(held) == i]
            for i in range(len(moves))
        ]

    def flip(v, ds):
        for d in ds:
            v = v + d - 2 * d * ((v // d) % 2)
        return v

    def jcols(j):
        return pl.ds(pl.multiple_of(j * CK, CK), CK)

    def xcols(k):
        return pl.ds(pl.multiple_of(k * XK, XK), XK)

    def remote(src, dst, ss, rs, device):
        return pltpu.make_async_remote_copy(
            src_ref=src, dst_ref=dst, send_sem=ss, recv_sem=rs,
            device_id=device, device_id_type=MESH,
        )

    def loop(n, fn):
        def step(i, carry):
            fn(i)
            return carry
        lax.fori_loop(0, n, step, 0)

    def wout_copy(k):
        return pltpu.make_async_copy(wout_hbm.at[0, :, xcols(k)], wout.at[:, xcols(k)], wout_sem.at[k])

    def wqkv_copy(j):
        return pltpu.make_async_copy(
            wqkv_hbm.at[0, :, jcols(j), :], wqkv.at[:, jcols(j), :], wqkv_sem.at[j]
        )

    def xhop(m, section):
        return remote(xs.at[0, m], xfull.at[m, c, z], xh_s.at[m], xh_r.at[m], (section, t))

    def xmove(m, k, d, n, held):
        ref = xfull.at[m, c, flip(z, held), :, xcols(k)]
        return remote(ref, ref, xa_s.at[m, k, n], xa_r.at[m, k, n], (s, flip(z, (d,)) * 2 + c))

    def xmove_in(m, k, d, n, held):
        ref = xfull.at[m, c, flip(flip(z, (d,)), held), :, xcols(k)]
        return remote(ref, ref, xa_s.at[m, k, n], xa_r.at[m, k, n], (s, flip(z, (d,)) * 2 + c))

    def lend(m, k, n, ds):
        return remote(
            cot.at[m, :, xcols(k)], xfull.at[m, c, z, :, xcols(k)],
            ln_s.at[m, k, n], xa_r.at[m, k, n], (S - 1, flip(z, ds) * 2 + c),
        )

    def lent(m, k):
        return last & ((m > 0) | (k >= KA))

    def lends(m, k):
        if m > 0:
            return S - 3
        return S - 2 - k % 2

    def xsib(m, k):
        ref = xfull.at[m, c, :, :, xcols(k)]
        return remote(ref, ref, xs_s.at[m, k], xs_r.at[m, k], (s, sib))

    def xsib_in(m, k):
        ref = xfull.at[m, 1 - c, :, :, xcols(k)]
        return remote(ref, ref, xs_s.at[m, k], xs_r.at[m, k], (s, sib))

    def hop(u, j, section):
        return remote(
            gout.at[u, j], full.at[u, j, c, z], hop_s.at[u, j], hop_r.at[u, j], (section, t)
        )

    def gmove(u, j, n, ds, held):
        ref = full.at[u, j, c, flip(z, held)]
        return remote(ref, ref, g_s.at[u, j, n], g_r.at[u, j, n], (s, flip(z, ds) * 2 + c))

    def gmove_in(u, j, n, ds, held):
        ref = full.at[u, j, c, flip(flip(z, ds), held)]
        return remote(ref, ref, g_s.at[u, j, n], g_r.at[u, j, n], (s, flip(z, ds) * 2 + c))

    def sg_out(u, j):
        ref = full.at[u, j, c]
        return remote(ref, ref, sg_s.at[u, j], sg_r.at[u, j], (s, sib))

    def sg_in(u, j):
        ref = full.at[u, j, 1 - c]
        return remote(ref, ref, sg_s.at[u, j], sg_r.at[u, j], (s, sib))

    def rb(u, j):
        return remote(part.at[u, j, 1 - c], sibs.at[u, j], rb_s.at[u, j], rb_r.at[u, j], (s, sib))

    def rz(u, j, d, n, held):
        q = flip(z, (d,))
        return remote(
            part.at[u, j, c, flip(q, held)], zgot.at[u, j, n],
            rz_s.at[u, j, n], rz_r.at[u, j, n], (s, q * 2 + c),
        )

    def ci_out(u, o, section):
        return remote(dsend.at[u], coefin.at[u, t], ci_s.at[u, o], ci_r.at[u], (section, o))

    def ci_in(u):
        return remote(coefin.at[u], coefin.at[u], ci_s.at[u, 0], ci_r.at[u], (s, sib))

    barrier = pltpu.get_barrier_semaphore()
    for dt in range(1, T):
        pl.semaphore_signal(barrier, inc=1, device_id=(s, lax.rem(t + dt, T)), device_id_type=MESH)

    @pl.when(s > 0)
    def _():
        for o in range(T):
            pl.semaphore_signal(barrier, inc=1, device_id=(s - 1, o), device_id_type=MESH)

    @pl.when(s < S - 1)
    def _():
        for o in range(T):
            pl.semaphore_signal(barrier, inc=1, device_id=(s + 1, o), device_id_type=MESH)

    @pl.when(last)
    def _():
        for o in range(T):
            pl.semaphore_signal(barrier, inc=1, device_id=(S - 3, o), device_id_type=MESH)

    loop(KX, lambda k: wout_copy(k).start())
    loop(J, lambda j: wqkv_copy(j).start())

    @pl.when(last)
    def _():
        for m in range(M):
            xfull[m, c, z] = cot[m]

    ends = jnp.where(s == 0, 1, 0) + jnp.where(s == S - 1, 1, 0)
    pl.semaphore_wait(barrier, T - 1 + T * (2 - ends) + jnp.where(s == S - 3, T, 0))

    def move_start(m, i):
        d, pieces = moves[i]

        def one(k):
            @pl.when(~lent(m, k))
            def _():
                if i > 0:
                    before, arrived = moves[i - 1]
                    for n, held in arrived:
                        xmove_in(m, k, before, n, held).wait_recv()
                for n, held in pieces:
                    xmove(m, k, d, n, held).start()

        loop(KX, one)

    def move_end(m):
        before, arrived = moves[-1]

        def one(k):
            for n, held in arrived:
                xmove_in(m, k, before, n, held).wait_recv()

            @pl.when(lent(m, k))
            def _():
                for d, pieces in moves[:-1]:
                    for n, held in pieces:
                        xmove_in(m, k, d, n, held).wait_recv()

            xsib(m, k).start()

        loop(KX, one)

    def multiply(m):
        ymat[m] = jnp.zeros((L, C), f32)

        def one(k):
            @pl.when(m == 0)
            def _():
                wout_copy(k).wait()

            xsib_in(m, k).wait_recv()
            rows = jnp.concatenate([xfull[m, o % 2, o // 2, :, xcols(k)] for o in range(T)], axis=0)
            ymat[m] += mm(rows, wout[:, xcols(k)], NT)

        loop(KX, one)

    def lending(fn, units):
        for m in units:
            for k in range(KX):
                if m > 0 or k >= KA:
                    @pl.when(s == lends(m, k))
                    def _():
                        for n, ds in spans:
                            fn(m, k, n, ds)

    @pl.when(last)
    def _():
        move_start(0, 0)

    lending(lambda m, k, n, ds: lend(m, k, n, ds).start(), range(0, 1))

    @pl.when(s > 0)
    def _():
        for m in range(M):
            xhop(m, s - 1).start()

    lending(lambda m, k, n, ds: lend(m, k, n, ds).wait_send(), range(0, 1))
    lending(lambda m, k, n, ds: lend(m, k, n, ds).start(), range(1, M))

    def prepare(u):
        nb = layout.shape[1]
        bl = L // nb
        kb = lax.broadcasted_iota(jnp.int32, (bl, L), 1) // bl
        strips = []
        for b in range(nb):
            strip = kb == layout[u, b, 0]
            for e in range(1, layout.shape[2]):
                strip = strip | (kb == layout[u, b, e])
            strips.append(jnp.where(strip, 1.0, 0.0))
        listed = jnp.concatenate(strips, axis=0)
        row = lax.broadcasted_iota(jnp.int32, (L, L), 0)
        col = lax.broadcasted_iota(jnp.int32, (L, L), 1)
        allowed = (listed > 0.5) & (col <= row)
        for h in range(C // HD):
            hc = slice(h * HD, (h + 1) * HD)
            scores = jnp.where(allowed, mm(qs[u, :, hc], ks[u, :, hc], NT) * scale, -1e30)
            expo = jnp.exp(scores - jnp.max(scores, axis=1, keepdims=True))
            probs = expo / jnp.sum(expo, axis=1, keepdims=True)
            probs_keep[u, h] = probs
            att_keep[u, :, hc] = mm(probs.astype(bf), vs[u, :, hc], NN)

    for m in range(M):
        def square(k, carry):
            x = xs[0, m, :, xcols(k)].astype(f32)
            return carry + jnp.sum(x * x, axis=1, keepdims=True)

        squares = lax.fori_loop(0, KX, square, jnp.zeros((R, 1), f32))
        factor[m] = jnp.broadcast_to(lax.rsqrt(squares / D + 1e-05), (R, LANE))

    prepare(0)

    @pl.when(last)
    def _():
        for i in range(1, len(moves)):
            move_start(0, i)

    for m in range(1, M):
        prepare(m)

    @pl.when(last)
    def _():
        move_end(0)
        multiply(0)

    @pl.when(s < S - 1)
    def _():
        for m in range(M):
            xhop(m, s).wait_recv()
            move_start(m, 0)
        for i in range(1, len(moves)):
            for m in range(M):
                move_start(m, i)
        move_end(0)
        multiply(0)

    @pl.when(s < S - 2)
    def _():
        for m in range(1, M):
            move_end(m)
            multiply(m)

    def attend(u):
        @pl.when(last)
        def _():
            coef[...] = jnp.full((L, LANE), -1.0, f32)

        @pl.when(s < S - 1)
        def _():
            ci_in(u).wait_recv()
            coef[...] = jnp.concatenate([coefin[u, o] for o in range(T)], axis=0)

        for h in range(C // HD):
            hc = slice(h * HD, (h + 1) * HD)
            query = qs[u, :, hc]
            key = ks[u, :, hc]
            value = vs[u, :, hc]
            go = (acc[:, hc] - coef[...] * ymat[u, :, hc]).astype(bf)
            probs = probs_keep[u, h]
            delta = jnp.sum(att_keep[u, :, hc] * go.astype(f32), axis=1, keepdims=True)
            dprob = mm(go, value, NT)
            dscore = (probs * (dprob - delta)).astype(bf)
            grads[0, :, hc] = (mm(dscore, key, NN) * scale).astype(bf)
            grads[1, :, hc] = (mm(dscore, query, TN) * scale).astype(bf)
            grads[2, :, hc] = mm(probs.astype(bf), go, TN).astype(bf)
        dacc[...] = jnp.zeros_like(dacc)

    def produce(u, j):
        @pl.when(u == 0)
        def _():
            wqkv_copy(j).wait()

        cols = jcols(j)
        value = mm(grads[0], wqkv[0, cols, :], NT)
        value = value + mm(grads[1], wqkv[1, cols, :], NT)
        value = value + mm(grads[2], wqkv[2, cols, :], NT)
        value = value.astype(bf)
        for o in range(T):
            part[u, j, o % 2, o // 2] = value[o * R : (o + 1) * R]
        rb(u, j).start()

    def combine(u, j, i):
        if i == 0:
            rb(u, j).wait_recv()
            part[u, j, c] = (part[u, j, c].astype(f32) + sibs[u, j].astype(f32)).astype(bf)
        else:
            before, arrived = halves[i - 1]
            for n, held in arrived:
                rz(u, j, before, n, held).wait_recv()
            for n, held in arrived:
                if held:
                    at = flip(z, held)
                    total = part[u, j, c, at].astype(f32) + zgot[u, j, n].astype(f32)
                    part[u, j, c, at] = total.astype(bf)
        d, pieces = halves[i]
        for n, held in pieces:
            rz(u, j, d, n, held).start()

    def finish(u, j):
        before, arrived = halves[-1]
        for n, held in arrived:
            rz(u, j, before, n, held).wait_recv()
        cols = jcols(j)
        total = part[u, j, c, z].astype(f32)
        for d, pieces in halves:
            total = total + zgot[u, j, pieces[0][0]].astype(f32)
        scaled = total * gain[:, cols]
        mine = coef[pl.ds(pl.multiple_of(t * R, R), R), :][:, 0:1]
        above = xfull[u, c, z, :, cols].astype(f32)
        came = jnp.where(last, 0.0, full[u, j, c, z].astype(f32))
        value = came - mine * above + factor[u][:, 0:1] * scaled
        keep[u, :, cols] = value

        @pl.when(s > 0)
        def _():
            gout[u, j] = value.astype(bf)
            hop(u, j, s - 1).start()

        product = scaled * xs[0, u, :, cols].astype(f32)
        sums = product[:, 0:LANE]
        for i in range(1, CK // LANE):
            sums = sums + product[:, i * LANE : (i + 1) * LANE]
        dacc[...] += sums

    def settle(u):
        r = factor[u]
        dots = jnp.sum(dacc[...], axis=1, keepdims=True)
        dsend[u] = r * r * dots * (1.0 / D)

        @pl.when(s > 0)
        def _():
            for o in range(T):
                ci_out(u, o, s - 1).start()

    def give(u):
        cc = dsend[u][:, 0:1]

        def one(j):
            cols = jcols(j)
            out[u, :, cols] = (keep[u, :, cols] - cc * xs[0, u, :, cols].astype(f32)).astype(bf)

        loop(J, one)

    def spread(u, j, i):
        if i == 0:
            hop(u, j, s).wait_recv()
        else:
            arrived = [v for v in gmoves[i - 1] if i == len(gmoves) or v[1] != (1,)]
            if i == len(gmoves):
                arrived = arrived + [v for moved in gmoves[:-1] for v in moved if v[1] == (1,)]
            for move in arrived:
                gmove_in(u, j, *move).wait_recv()
        if i < len(gmoves):
            for move in gmoves[i]:
                gmove(u, j, *move).start()
        else:
            sg_out(u, j).start()

    def project(u, j):
        sg_in(u, j).wait_recv()
        rows = jnp.concatenate([full[u, j, o % 2, o // 2] for o in range(T)], axis=0)
        acc[...] += mm(rows, wout[:, jcols(j)], NT)

    P1, PD, QA, QB, QD = SKEW
    PE = P1 + PD * len(halves)
    Q0 = jnp.where(s == S - 2, QA, QB)
    QE = Q0 + QD * (len(gmoves) + 1)
    steps = J + max(PE, max(QA, QB) + QD * (len(gmoves) + 1))

    def merged(n):
        u = n - 1
        mine = u >= 0
        more = u + 1 < M

        @pl.when((s >= S - 2) & (u > 0))
        def _():
            multiply(u)

        @pl.when(mine)
        def _():
            attend(u)

        acc[...] = jnp.zeros_like(acc)

        def step(i):
            def on(skew):
                return (i >= skew) & (i < J + skew)

            @pl.when(mine)
            def _():
                @pl.when(i < J)
                def _():
                    produce(u, i)

                for k in range(len(halves)):
                    @pl.when(on(P1 + PD * k))
                    def _():
                        combine(u, i - (P1 + PD * k), k)

                @pl.when(on(PE))
                def _():
                    finish(u, i - PE)

                @pl.when(i == J + PE - 1)
                def _():
                    settle(u)
                    give(u)

            @pl.when(more & (s < S - 1))
            def _():
                for k in range(len(gmoves) + 1):
                    @pl.when(on(Q0 + QD * k))
                    def _():
                        spread(u + 1, i - (Q0 + QD * k), k)

                @pl.when(on(QE))
                def _():
                    project(u + 1, i - QE)

        loop(steps, step)

        @pl.when((s >= S - 2) & mine & more)
        def _():
            move_end(u + 1)

    loop(M + 1, merged)

    lending(lambda m, k, n, ds: lend(m, k, n, ds).wait_send(), range(1, M))

    @pl.when(s > 0)
    def _():
        for m in range(M):
            xhop(m, s - 1).wait_send()

    def drain(m):
        def drain_k(k):
            @pl.when(~lent(m, k))
            def _():
                for d, pieces in moves:
                    for n, held in pieces:
                        xmove(m, k, d, n, held).wait_send()

            xsib(m, k).wait_send()

        loop(KX, drain_k)

        def drain_j(j):
            rb(m, j).wait_send()
            for d, pieces in halves:
                for n, held in pieces:
                    rz(m, j, d, n, held).wait_send()

            @pl.when(s < S - 1)
            def _():
                for moved in gmoves:
                    for move in moved:
                        gmove(m, j, *move).wait_send()
                sg_out(m, j).wait_send()

            @pl.when(s > 0)
            def _():
                hop(m, j, s - 1).wait_send()

        loop(J, drain_j)

        @pl.when(s > 0)
        def _():
            for o in range(T):
                ci_out(m, o, s - 1).wait_send()

    loop(M, drain)


def solution(mesh):
    S = mesh.shape["pipe"]
    T = mesh.shape["tensor"]

    def shards(cotangent, inputs, norm_gain, queries, keys, values, qkv_weight, out_weight, layout):
        M, R, D = cotangent.shape
        C = queries.shape[3]
        L = queries.shape[2]
        Z = T // 2
        J = 8
        KX = 4
        KA = 2
        DIRECT = False
        SKEW = (1, 2, 9, 12, 2)
        CK = D // J
        sizes = (S, T, M, R, D, C, L, J, KX, KA, DIRECT, SKEW)
        vmem = pl.BlockSpec(memory_space=pltpu.VMEM)
        hbm = pl.BlockSpec(memory_space=pl.ANY)
        bf = jnp.bfloat16
        f32 = jnp.float32
        dma = pltpu.SemaphoreType.DMA
        V = pltpu.VMEM
        result = pl.pallas_call(
            functools.partial(body, sizes),
            out_shape=jax.ShapeDtypeStruct((M, R, D), bf),
            in_specs=[pl.BlockSpec(memory_space=pltpu.SMEM)] + [vmem] * 6 + [hbm] * 2,
            out_specs=vmem,
            scratch_shapes=[
                V((3, D, C), bf),
                V((C, D), bf),
                V((M, 2, Z, R, D), bf),
                V((M, J, 2, Z, R, CK), bf),
                V((M, J, 2, Z, R, CK), bf),
                V((M, J, Z, R, CK), bf),
                V((M, J, Z - 1, R, CK), bf),
                V((M, J, R, CK), bf),
                V((M, R, D), f32),
                V((M, L, C), f32),
                V((L, C), f32),
                V((3, L, C), bf),
                V((M, C // HD, L, L), f32),
                V((M, L, C), f32),
                V((L, LANE), f32),
                V((M, R, LANE), f32),
                V((R, LANE), f32),
                V((M, R, LANE), f32),
                V((M, T, R, LANE), f32),
                dma((KX,)),
                dma((J,)),
                dma((M, KX, Z - 1)),
                dma((M,)),
                dma((M,)),
                dma((M, KX, Z - 1)),
                dma((M, KX, Z - 1)),
                dma((M, KX)),
                dma((M, KX)),
                dma((M, J)),
                dma((M, J)),
                dma((M, J, Z - 1)),
                dma((M, J, Z - 1)),
                dma((M, J)),
                dma((M, J)),
                dma((M, J)),
                dma((M, J)),
                dma((M, J, Z - 1)),
                dma((M, J, Z - 1)),
                dma((M, T)),
                dma((M,)),
            ],
            compiler_params=pltpu.CompilerParams(
                collective_id=0, has_side_effects=True, vmem_limit_bytes=62 * 1024 * 1024
            ),
        )(
            layout, cotangent, inputs, norm_gain, queries[0], keys[0], values[0],
            qkv_weight, out_weight,
        )
        return result[None]

    in_specs = (
        P(None, "tensor", None),
        P("pipe", None, "tensor", None),
        P("pipe", None),
        P("pipe", None, None, "tensor"),
        P("pipe", None, None, "tensor"),
        P("pipe", None, None, "tensor"),
        P("pipe", None, None, "tensor"),
        P("pipe", "tensor", None),
        P(),
    )
    out_specs = P("pipe", None, "tensor", None)
    return jax.shard_map(shards, mesh=mesh, in_specs=in_specs, out_specs=out_specs, check_vma=False)
```
